32 devices in a mesh: groups: 2 (over y), section: 2 (over core), row: 2 (over x), col: 4 (over z).
Axes of the slice: x: 2, y: 2, z: 4, core: 2. Of those that a mesh axis runs over, the one named last changes fastest.
Arguments:
- hidden: bfloat16 [2, 2, 3072, 8192], P('section', None, ('groups', 'col'), 'row'), parts along dimension 2, may hold values from -400 to 400
- upstream: bfloat16 [2, 3072, 8192], P(None, ('groups', 'col'), 'row'), parts along dimension 1, may hold values from -8 to 8
- weights: bfloat16 [2, 8192, 8192], P('section', 'row', 'col'), may hold values from -0.0625 to 0.0625
- norm_gains: bfloat16 [2, 8192], P('section', 'row'), may hold values from 0.5 to 1.5
- steering: bfloat16 [16384], P(('groups', 'row')), parts along dimension 0, may hold values from -18 to 18
- steer_layer: int32 [2, 3072], P(None, ('groups', 'col')), parts along dimension 1, may hold values from 0 to 1
Outputs:
- section_grads: bfloat16 [2, 2, 3072, 8192], P('section', None, ('groups', 'col'), 'row'), parts along dimension 2
- steer_grad: float32 [16384], P(('groups', 'row')), parts along dimension 0
The draws below stay inside these ranges and needn't reach their ends.
There are 2 independent parts, one for each index of `groups`. The reference program is written for one: setup_inputs(seed, part) draws one part's arguments, and reference() takes and returns one part's arrays. A program takes and returns all parts, laid end to end along the dimension named above; an argument that names none is the same for every part. Nothing has to cross between parts.
All inputs are finite; a program needn't handle non-finite values.
Results may differ from the reference program's by a relative error of at most 0.0038.
Values may be sent and summed in bfloat16 or wider, within the bound.
A program may use at most 320 MiB of HBM per device.

```python
import math
import jax
import jax.numpy as jnp
from jax import lax

D = 8192
ROWS = 1536
MICRO = 2
SECTIONS = 2


def shared_parts(key):
    key_common, key_column, key_scale = jax.random.split(jax.random.fold_in(key, 101), 3)
    common = jnp.clip(jax.random.normal(key_common, (MICRO, ROWS, D), jnp.float32), -5.0, 5.0)
    row_scale = jnp.exp(jax.random.uniform(key_scale, (MICRO, ROWS, 1), jnp.float32, math.log(0.3), math.log(3.0)))
    column = jnp.exp(jax.random.uniform(key_column, (D,), jnp.float32, 0.0, math.log(10.0)))
    return (common, column, row_scale)


def draw_hidden(key, part):
    common, column, row_scale = shared_parts(key)
    own = jnp.clip(jax.random.normal(jax.random.fold_in(key, 202), (SECTIONS, MICRO, ROWS, D), jnp.float32), -5.0, 5.0)
    values = (common[None] + 0.7 * own) * column * row_scale[None]
    return values.astype(jnp.bfloat16)


def draw_upstream(key, part):
    common, column, row_scale = shared_parts(key)
    noise = jnp.clip(jax.random.normal(jax.random.fold_in(key, 303), (MICRO, ROWS, D), jnp.float32), -5.0, 5.0)
    return (noise + 0.5 * common).astype(jnp.bfloat16)


def set_ends(result, own_key, smallest, largest):
    shape = result.shape
    place = [jax.random.randint(jax.random.fold_in(own_key, axis), (), 0, shape[axis]) for axis in range(len(shape))]
    result = result.at[tuple(place)].set(smallest)
    longest = shape.index(max(shape))
    place[longest] = (place[longest] + 1) % shape[longest]
    return result.at[tuple(place)].set(largest)


def block_levels(own_key, shape, pieces, smallest, largest):
    loudness, own = 1.0, jax.random.fold_in(own_key, 6)
    for dim, shards_of in pieces:
        heights = jnp.exp(jax.random.uniform(jax.random.fold_in(own, dim), (shards_of,), jnp.float32, smallest / len(pieces), largest / len(pieces)))
        loudness = loudness * jnp.repeat(heights, shape[dim] // shards_of).reshape([-1 if axis == dim else 1 for axis in range(len(shape))])
    return loudness


def normal_values(stream_key, dims, width, bound, shards=(), kind=jnp.bfloat16):
    array = jax.random.normal(stream_key, dims, jnp.float32) * width
    if len(shards) > 0:
        array = block_levels(stream_key, dims, shards, -0.22, 0.18) * array
    return jnp.clip(array, min=-bound, max=bound).astype(kind)


def setup_inputs(seed: int = 0, part: int = 0) -> dict:
    arg_keys = jax.random.split(jax.random.key(seed), 7)
    part_keys = jax.random.split(jax.random.fold_in(arg_keys[6], part), 7)
    return {
        "hidden": draw_hidden(jax.random.fold_in(jax.random.fold_in(arg_keys[6], part), 71), part),
        "upstream": draw_upstream(jax.random.fold_in(jax.random.fold_in(arg_keys[6], part), 71), part),
        "weights": normal_values(arg_keys[2], (SECTIONS, D, D), D ** -0.5, 0.0625, ((0, 2), (1, 2), (2, 4))),
        "norm_gains": jnp.clip(1.0 + 0.1 * jax.random.normal(arg_keys[3], (SECTIONS, D), jnp.float32), 0.5, 1.5).astype(jnp.bfloat16),
        "steering": normal_values(part_keys[4], (D,), 3.0, 18.0, ((0, 2),)),
        "steer_layer": set_ends(jax.random.randint(part_keys[5], (MICRO, ROWS), 0, SECTIONS), jax.random.fold_in(part_keys[5], 1), 0, SECTIONS - 1).astype(jnp.int32),
    }


epsilon = 1e-06

def reference(hidden, upstream, weights, norm_gains, steering, steer_layer):
    steer_vec = steering.astype(jnp.float32)
    incoming = [upstream[micro_index] for micro_index in range(MICRO)]
    section_blocks = [None] * SECTIONS
    steer_sum = jnp.zeros((D,), jnp.float32)
    for section_index in reversed(range(SECTIONS)):
        scaling = norm_gains[section_index].astype(jnp.float32)
        passed_list = []
        for micro_index in range(MICRO):
            steered = (steer_layer[micro_index] == section_index)[:, None]
            unsteered = hidden[section_index, micro_index].astype(jnp.float32)
            moved = unsteered + steer_vec
            norm_plain = jnp.sqrt(lax.optimization_barrier(jnp.sum(unsteered * unsteered, -1, keepdims=True)) + epsilon)
            norm_moved = jnp.sqrt(lax.optimization_barrier(jnp.sum(moved * moved, -1, keepdims=True)) + epsilon)
            rescale = norm_plain / norm_moved
            rescaled = jnp.where(steered, moved * rescale, unsteered)
            root_mean = jnp.sqrt(lax.optimization_barrier(jnp.mean(rescaled * rescaled, -1, keepdims=True)) + epsilon)
            grad_float = incoming[micro_index].astype(jnp.float32)
            normal_grad = jnp.dot(incoming[micro_index], weights[section_index].T, preferred_element_type=jnp.float32)
            scaled = scaling * normal_grad
            curvature = lax.optimization_barrier(jnp.sum(scaled * rescaled, -1, keepdims=True))
            input_grad = grad_float + scaled / root_mean - rescaled * curvature / (D * root_mean ** 3)
            direction = moved / norm_moved
            radial = lax.optimization_barrier(jnp.sum(direction * input_grad, -1, keepdims=True))
            tangent = rescale * (input_grad - direction * radial)
            below = jnp.where(steered, tangent + unsteered / norm_plain * radial, input_grad)
            steer_sum = steer_sum + lax.optimization_barrier(jnp.sum(jnp.where(steered, tangent, 0.0), 0))
            passed_list.append(below.astype(jnp.bfloat16))
        incoming = passed_list
        section_blocks[section_index] = jnp.stack(passed_list)
    return (jnp.stack(section_blocks), steer_sum / (MICRO * ROWS))
```

```python
import jax
import jax.numpy as jnp
from jax import lax
from jax.experimental import pallas as pl
from jax.experimental.pallas import tpu as pltpu
from jax.sharding import PartitionSpec as P

D = 8192
ROWS = 1536
MICRO = 2


epsilon = 1e-06
MESH = pl.DeviceIdType.MESH


def shifted(value, axis, steps=1):
    count = lax.axis_size(axis)
    return lax.ppermute(value, axis, [(source, (source + steps) % count) for source in range(count)])


def columns(value, start, width):
    return lax.dynamic_slice_in_dim(value, start, width, value.ndim - 1)


def after(value, earlier):
    return lax.optimization_barrier((value, earlier))[0]


def local(hidden, upstream, weights, norm_gains, steering, steer_layer):
    core = lax.axis_index("section")
    row_index = lax.axis_index("row")
    col_index = lax.axis_index("col")
    group = lax.axis_index("groups")
    row_devices = lax.axis_size("row")
    cols = lax.axis_size("col")
    groups = lax.axis_size("groups")
    micro, row_count, features = upstream.shape
    tokens = micro * row_count
    half = features // 2
    depth = weights.shape[2]
    part = depth // groups
    f32 = jnp.float32

    def own_columns(value):
        return columns(value, core * half, half)

    def per_section(mine, received):
        return jnp.where(core == 0, mine, received), jnp.where(core == 1, mine, received)

    def over_cores(value, axis):
        mine = lax.dynamic_slice_in_dim(value, core * half, half, axis)
        given = lax.dynamic_slice_in_dim(value, (1 - core) * half, half, axis)
        return per_section(mine, shifted(given, "section"))

    units = max(1, part // 128)
    step_units = max(1, units // 4)
    unit = part // units
    widths_of = {}
    for section in (1, 0):
        sizes = [step_units] * (units // step_units)
        if sum(sizes) < units:
            sizes.append(units - sum(sizes))
        widths_of[section] = [size * unit for size in sizes]
    mine = lax.dynamic_slice_in_dim(weights[0], core * half, half, 0)
    given = lax.dynamic_slice_in_dim(weights[0], (1 - core) * half, half, 0)
    lead = sum(widths_of[1][:2])
    lead_given = shifted(columns(given, group * part, lead), "section")
    first_pieces = per_section(columns(mine, group * part, lead), lead_given)
    weight_of = per_section(mine, shifted(after(given, lead_given), "section"))
    hidden_of = over_cores(hidden[0].reshape(tokens, features), 1)
    gain_of = over_cores(norm_gains[0], 0)
    steer_vec = own_columns(steering).astype(f32)
    layers = steer_layer.reshape(tokens)
    upstream_rows = upstream.reshape(tokens, features)

    earlier, sent = [], []
    pieces = {}
    for section in (1, 0):
        held = []
        start = 0
        for width in widths_of[section]:
            if start + width <= lead:
                own = first_pieces[section][:, start : start + width]
            else:
                own = columns(weight_of[section], group * part + start, width)
            if earlier:
                own = after(own, tuple(earlier))
            gathered = lax.all_gather(own, "col", axis=1, tiled=True)
            others = jnp.concatenate(
                [columns(gathered, ((col_index + step) % cols) * width, width) for step in range(1, cols)], 1
            )
            held.append((start, width, (others, shifted(others, "groups"))))
            earlier = [others] + sent[-1:]
            sent.append(held[-1][2][1])
            start += width
        pieces[section] = held

    def projected(full, section):
        def times(left, right):
            return lax.dot_general(left, right, (((1,), (1,)), ((), ())), preferred_element_type=f32)

        total = times(columns(full, col_index * depth, depth), weight_of[section])
        held = pieces[section]
        for start, width, sides in held:
            total = lax.optimization_barrier(total)
            for side, block in enumerate(sides):
                offset = ((group + side) % groups) * part + start
                left = jnp.concatenate(
                    [columns(full, ((col_index + step) % cols) * depth + offset, width) for step in range(1, cols)], 1
                )
                total = total + times(left, block)
        return total

    def all_features(own):
        if row_devices == 2:
            other = shifted(own, "row")
            both = jnp.concatenate([jnp.where(row_index == 0, own, other), jnp.where(row_index == 0, other, own)], 1)
            if own.shape[1] == features:
                return both
            there = shifted(both, "section")
            lower = jnp.where(core == 0, both, there)
            upper = jnp.where(core == 0, there, both)
            return jnp.concatenate([lower[:, :half], upper[:, :half], lower[:, half:], upper[:, half:]], 1)
        if own.shape[1] == features:
            return lax.all_gather(own, "row", axis=1, tiled=True)
        return lax.all_gather(own, ("row", "section"), axis=1, tiled=True)

    local_sums = []
    for section in range(2):
        unsteered = hidden_of[section].astype(f32)
        moved = unsteered + steer_vec
        local_sums += [jnp.sum(unsteered * unsteered, -1), jnp.sum(moved * moved, -1)]
    sums = lax.psum(tuple(local_sums), ("row", "section"))

    incoming = own_columns(upstream_rows)
    full = all_features(upstream_rows)
    steer_part = jnp.zeros((half,), f32)
    blocks = [None, None]
    for section in (1, 0):
        plain_sq, moved_sq = sums[2 * section], sums[2 * section + 1]
        steered = layers == section
        steered_col = steered[:, None]
        unsteered = hidden_of[section].astype(f32)
        moved = unsteered + steer_vec
        grad_float = incoming.astype(f32)
        scaled = gain_of[section].astype(f32) * projected(full, section)
        chosen = jnp.where(steered_col, moved, unsteered)
        curve, inner = lax.psum(
            (jnp.sum(scaled * chosen, -1), jnp.sum(grad_float * moved, -1)), ("row", "section")
        )
        norm_plain = jnp.sqrt(plain_sq + epsilon)
        norm_moved = jnp.sqrt(moved_sq + epsilon)
        rescale = norm_plain / norm_moved
        square_sum = jnp.where(
            steered, norm_plain * norm_plain * moved_sq / (norm_moved * norm_moved), plain_sq
        )
        root_mean = jnp.sqrt(square_sum / D + epsilon)
        scale = jnp.where(steered, rescale, 1.0)
        factor = scale * curve / (D * root_mean**3)
        input_grad = grad_float + scaled / root_mean[:, None] - chosen * (scale * factor)[:, None]
        radial = (inner + curve / root_mean - rescale * factor * moved_sq) / norm_moved
        tangent = rescale[:, None] * (input_grad - moved * (radial / norm_moved)[:, None])
        below = jnp.where(steered_col, tangent + unsteered * (radial / norm_plain)[:, None], input_grad)
        passed = below.astype(jnp.bfloat16)
        blocks[section] = passed
        steer_part = steer_part + jnp.sum(jnp.where(steered_col, tangent, 0.0), 0)
        if section == 1:
            incoming = passed
            full = all_features(passed)
    kept = jnp.where(core == 0, blocks[0], blocks[1])
    received = shifted(jnp.where(core == 0, blocks[1], blocks[0]), "section")
    lower = jnp.where(core == 0, kept, received)
    upper = jnp.where(core == 0, received, kept)
    result = jnp.concatenate([lower, upper], 1).reshape(1, micro, row_count, features)
    steer_own = lax.psum(steer_part, "col")
    steer_other = shifted(steer_own, "section")
    steer_total = jnp.concatenate(
        [jnp.where(core == 0, steer_own, steer_other), jnp.where(core == 0, steer_other, steer_own)]
    )
    return (result, steer_total / (MICRO * ROWS))


CHUNKS = 3


def chunk_rows(part):
    widths = [part * 3 // 8, part * 3 // 8, part // 4]
    return [(0, widths[0]), (widths[0], widths[1]), (widths[0] + widths[1], widths[2])]


def relay_kernel(
    u, w, n1, wg, q, xc, w1, partial, total, got, own_sem, w1_sem, half_send, x1_send, x1_recv, a_send, a_recv,
    a_local, x2_send, x2_recv, c_send, c_recv, f_send, f_recv, wr_send, wr_recv, wl_send, wl_recv, y_send, y_recv,
    r_send, r_recv, l_send, l_recv, out_sem
):
    core, row, col, group = (lax.axis_index(name) for name in ("section", "row", "col", "groups"))
    micro, row_count, features = u.shape
    half = features // 2
    part = half // 2
    quarter = row_count // 4
    cols = 4
    last = cols - 1
    f32 = jnp.float32
    chunks = chunk_rows(part)

    barrier = pltpu.get_barrier_semaphore()
    peers = [{"col": (col + step) % cols} for step in range(1, cols)]
    peers += [{"row": 1 - row}, {"groups": 1 - group}, {"section": 1 - core}]
    for peer in peers:
        pl.semaphore_signal(barrier, inc=1, device_id=peer, device_id_type=MESH)
    pl.semaphore_wait(barrier, len(peers))

    late = []

    class Send:
        def __init__(self, src, dst, send, recv, device, when=None):
            self.copy = pltpu.make_async_remote_copy(
                src_ref=src, dst_ref=dst, send_sem=send, recv_sem=recv, device_id=device, device_id_type=MESH
            )
            self.when = when
            self.waited = False
            late.append(self)
            self.guarded(self.copy.start)

        def guarded(self, action):
            if self.when is None:
                action()
            else:
                pl.when(self.when)(lambda: action())

        def wait_send(self):
            if not self.waited:
                self.waited = True
                self.guarded(self.copy.wait_send)

    def arrived(ref, sem, when=None):
        copy = pltpu.make_async_remote_copy(
            src_ref=ref, dst_ref=ref, send_sem=sem, recv_sem=sem, device_id={"section": 1 - core}, device_id_type=MESH
        )
        if when is None:
            copy.wait_recv()
        else:
            pl.when(when)(lambda: copy.wait_recv())

    for order in range(2):
        h = (group + order) % 2
        mine, there = pl.ds(h * part, part), pl.ds(half + h * part, part)

        @pl.when(core == 0)
        def _():
            pltpu.make_async_remote_copy(
                src_ref=w.at[there], dst_ref=wg.at[col, mine], send_sem=half_send.at[order], recv_sem=own_sem.at[order],
                device_id={"section": 1 - core}, device_id_type=MESH,
            ).start()
            pltpu.make_async_copy(w.at[mine], wg.at[col, mine], own_sem.at[order]).start()

        @pl.when(core == 1)
        def _():
            pltpu.make_async_remote_copy(
                src_ref=w.at[mine], dst_ref=w1.at[mine], send_sem=half_send.at[order], recv_sem=w1_sem.at[order],
                device_id={"section": 1 - core}, device_id_type=MESH,
            ).start()
            pltpu.make_async_copy(w.at[there], w1.at[mine], w1_sem.at[order]).start()

    def wait_own(order):
        mine = pl.ds(((group + order) % 2) * part, part)
        pltpu.make_async_copy(w.at[mine], wg.at[col, mine], own_sem.at[order]).wait()

    def wait_w1(order):
        mine = pl.ds(((group + order) % 2) * part, part)
        pltpu.make_async_copy(w.at[mine], w1.at[mine], w1_sem.at[order]).wait()

    my_rows = pl.ds((row * 2 + core) * quarter, quarter)
    x1 = [
        Send(u.at[m, pl.ds(((1 - row) * 2 + core) * quarter, quarter)], q.at[m], x1_send.at[m], x1_recv.at[m], {"row": 1 - row})
        for m in range(micro)
    ]

    def columns_of(index):
        return pl.ds(pl.multiple_of((index % 2) * half, half), half)

    def to_cols(m, from_own):
        for step in range(cols):
            there = (col + step) % cols
            here = (there // 2) == row
            src = u.at[m, my_rows, columns_of(there)] if from_own else q.at[m, :, columns_of(there)]
            when = here if from_own else jnp.logical_not(here)
            dst = xc.at[m, col, my_rows]
            if step == 0:
                pl.when(when)(lambda: pltpu.make_async_copy(src, dst, a_local.at[m]).start())
            else:
                Send(src, dst, a_send.at[m, step, int(from_own)], a_recv.at[m, step], {"col": there}, when)

    z_sent = []

    def z_step(sends):
        z_sent.append(sends)
        if len(z_sent) > 2:
            for send in z_sent[-3]:
                send.wait_send()

    def w_rows(k):
        return pl.ds(pl.multiple_of(group * part + chunks[k][0], 128), chunks[k][1])

    def w_hop(hop, k):
        from_right, from_left = jnp.maximum(col - hop + 1, 0), jnp.minimum(col + hop - 1, last)
        return [
            Send(
                wg.at[from_right, w_rows(k)], wg.at[from_right, w_rows(k)], wr_send.at[hop - 1, k], wr_recv.at[hop - 1, k],
                {"col": jnp.minimum(col + 1, last)}, (col < last) & (col - hop + 1 >= 0),
            ),
            Send(
                wg.at[from_left, w_rows(k)], wg.at[from_left, w_rows(k)], wl_send.at[hop - 1, k], wl_recv.at[hop - 1, k],
                {"col": jnp.maximum(col - 1, 0)}, (col > 0) & (col + hop - 1 <= last),
            ),
        ]

    def w_arrived(hop, k):
        arrived(wg.at[jnp.maximum(col - hop, 0), w_rows(k)], wr_recv.at[hop - 1, k], col - hop >= 0)
        arrived(wg.at[jnp.minimum(col + hop, last), w_rows(k)], wl_recv.at[hop - 1, k], col + hop <= last)

    sources = [
        jnp.where(col == 0, 1, jnp.maximum(col - 1, 0)),
        (col + 2) % cols,
        jnp.where(col == 0, last, (col + 1) % cols),
    ]
    y_sent = []

    def y_swap(slot, k):
        if len(y_sent) > 1:
            y_sent[-2].wait_send()
        ref = wg.at[sources[slot], w_rows(k)]
        y_sent.append(Send(ref, ref, y_send.at[slot, k], y_recv.at[slot, k], {"groups": 1 - group}))

    def y_arrived(slot, k):
        rows = pl.ds(pl.multiple_of((1 - group) * part + chunks[k][0], 128), chunks[k][1])
        arrived(wg.at[sources[slot], rows], y_recv.at[slot, k])

    to_cols(0, True)
    wait_own(0)
    z_step(w_hop(1, 0))
    arrived(q.at[0], x1_recv.at[0])
    to_cols(0, False)
    to_cols(1, True)
    arrived(q.at[1], x1_recv.at[1])
    to_cols(1, False)

    def quarter_rows(row_at, core_at):
        return pl.ds((row_at * 2 + core_at) * quarter, quarter)

    def gather(m):
        for step in range(cols):
            source = (col - step) % cols
            ref = xc.at[m, source, my_rows]
            if step == 0:
                pltpu.make_async_copy(ref, ref, a_local.at[m]).wait()
            else:
                arrived(ref, a_recv.at[m, step])
            Send(ref, ref, x2_send.at[m, step], x2_recv.at[m, step], {"row": 1 - row})
            Send(ref, ref, c_send.at[m, step], c_recv.at[m, step], {"section": 1 - core})

    def gather_rest(m):
        for step in range(cols):
            ref = xc.at[m, (col - step) % cols, quarter_rows(1 - row, core)]
            arrived(ref, x2_recv.at[m, step])
            Send(ref, ref, f_send.at[m, step], f_recv.at[m, step], {"section": 1 - core})
        for step in range(cols):
            arrived(xc.at[m, (col - step) % cols, quarter_rows(row, 1 - core)], c_recv.at[m, step])
            arrived(xc.at[m, (col - step) % cols, quarter_rows(1 - row, 1 - core)], f_recv.at[m, step])

    tile = 512

    def multiply(m):
        @pl.loop(0, cols)
        def _(index):
            step = jnp.where(col == last, last - index, (index + 1) % cols)
            source = (col - step + cols) % cols

            @pl.loop(0, half // tile)
            def _(block):
                at = pl.ds(pl.multiple_of(block * tile, tile), tile)
                value = lax.dot_general(
                    xc[m, source], w1[at, :], (((1,), (1,)), ((), ())), preferred_element_type=f32
                )

                @pl.when(step == 0)
                def _():
                    total[m, :, at] = value

                @pl.when(step > 0)
                def _():
                    partial[m, jnp.maximum(step - 1, 0), :, at] = value.astype(jnp.bfloat16)

    def add(dst, src, when):
        @pl.when(when)
        def _():
            @pl.loop(0, row_count // 32)
            def _(block):
                at = pl.ds(pl.multiple_of(block * 32, 32), 32)
                dst[at, :] = (dst[at, :].astype(f32) + src[at, :].astype(f32)).astype(dst.dtype)

    def sums_step(m, tau):
        right, left = (col <= tau) & (col < last), (last - col <= tau) & (col > 0)
        to_right, to_left = partial.at[m, tau], partial.at[m, 2 - tau]
        if tau > 0:
            arrived(got.at[m, 0, tau - 1], r_recv.at[m, tau - 1], (col >= 1) & (col <= tau))
            add(to_right, got.at[m, 0, tau - 1], right & (col >= 1))
        sends = [
            Send(to_right, got.at[m, 0, tau], r_send.at[m, tau], r_recv.at[m, tau], {"col": jnp.minimum(col + 1, last)}, right)
        ]
        if tau > 0:
            arrived(got.at[m, 1, tau - 1], l_recv.at[m, tau - 1], (col < last) & (last - col <= tau))
            add(to_left, got.at[m, 1, tau - 1], left & (col < last))
        sends.append(
            Send(to_left, got.at[m, 1, tau], l_send.at[m, tau], l_recv.at[m, tau], {"col": jnp.maximum(col - 1, 0)}, left)
        )
        return sends

    def finish(m):
        arrived(got.at[m, 0, last - 1], r_recv.at[m, last - 1], col >= 1)
        add(total.at[m], got.at[m, 0, last - 1], col >= 1)
        arrived(got.at[m, 1, last - 1], l_recv.at[m, last - 1], col < last)
        add(total.at[m], got.at[m, 1, last - 1], col < last)
        pltpu.make_async_copy(total.at[m], n1.at[m], out_sem.at[m]).start()

    gather(0)
    z_step(w_hop(1, 1))
    gather_rest(0)
    w_arrived(1, 0)
    y_swap(0, 0)
    wait_w1(0)
    wait_w1(1)
    multiply(0)
    z_step(sums_step(0, 0) + w_hop(2, 0))
    gather(1)
    w_arrived(1, 1)
    y_swap(0, 1)
    z_step(sums_step(0, 1))
    gather_rest(1)
    multiply(1)
    w_arrived(2, 0)
    z_step(w_hop(3, 0))
    y_swap(1, 0)
    z_step(sums_step(1, 0) + w_hop(2, 1))
    z_step(sums_step(0, 2))
    w_arrived(3, 0)
    y_swap(2, 0)
    z_step(sums_step(1, 1))
    w_arrived(2, 1)
    z_step(w_hop(3, 1))
    y_swap(1, 1)
    finish(0)
    wait_own(1)
    z_step(sums_step(1, 2) + w_hop(1, 2))
    w_arrived(3, 1)
    y_swap(2, 1)
    w_arrived(1, 2)
    z_step(w_hop(2, 2))
    y_swap(0, 2)
    finish(1)
    w_arrived(2, 2)
    z_step(w_hop(3, 2))
    y_swap(1, 2)
    w_arrived(3, 2)
    y_swap(2, 2)
    for k in range(CHUNKS):
        for slot in range(3):
            y_arrived(slot, k)
    for send in late:
        send.wait_send()
    for order in range(2):
        pltpu.make_async_remote_copy(
            src_ref=w.at[pl.ds(0, part)], dst_ref=wg.at[col, pl.ds(0, part)], send_sem=half_send.at[order],
            recv_sem=own_sem.at[order], device_id={"section": 1 - core}, device_id_type=MESH,
        ).wait_send()
    for m in range(micro):
        pltpu.make_async_copy(total.at[m], n1.at[m], out_sem.at[m]).wait()


def relay(u, w):
    micro, row_count, features = u.shape
    half = features // 2
    dma = pltpu.SemaphoreType.DMA
    bf16 = jnp.bfloat16
    return pl.pallas_call(
        relay_kernel,
        out_shape=(
            jax.ShapeDtypeStruct((micro, row_count, half), jnp.float32),
            jax.ShapeDtypeStruct((4, half, half), bf16),
            jax.ShapeDtypeStruct((micro, row_count // 4, features), bf16),
        ),
        in_specs=[pl.BlockSpec(memory_space=pl.ANY)] * 2,
        out_specs=(pl.BlockSpec(memory_space=pl.ANY),) * 3,
        scratch_shapes=[
            pltpu.VMEM((micro, 4, row_count, half), bf16),
            pltpu.VMEM((half, half), bf16),
            pltpu.VMEM((micro, 3, row_count, half), bf16),
            pltpu.VMEM((micro, row_count, half), jnp.float32),
            pltpu.VMEM((micro, 2, 3, row_count, half), bf16),
            dma((2,)), dma((2,)), dma((2,)),
            dma((2,)), dma((2,)),
            dma((2, 4, 2)), dma((2, 4)), dma((2,)),
            dma((2, 4)), dma((2, 4)), dma((2, 4)), dma((2, 4)), dma((2, 4)), dma((2, 4)),
            dma((3, CHUNKS)), dma((3, CHUNKS)), dma((3, CHUNKS)), dma((3, CHUNKS)),
            dma((3, CHUNKS)), dma((3, CHUNKS)),
            dma((2, 3)), dma((2, 3)), dma((2, 3)), dma((2, 3)),
            dma((2,)),
        ],
        compiler_params=pltpu.CompilerParams(
            collective_id=0, has_side_effects=True, vmem_limit_bytes=62 * 1024 * 1024
        ),
        cost_estimate=pl.CostEstimate(
            flops=2 * micro * 4 * row_count * half * half, bytes_accessed=100 * 1024 * 1024, transcendentals=0
        ),
        name="relay",
    )(u, w)


def shared_weights(hidden, upstream, weights, norm_gains, steering, steer_layer):
    core = lax.axis_index("section")
    row = lax.axis_index("row")
    micro, row_count, features = upstream.shape
    tokens = micro * row_count
    half = features // 2
    f32 = jnp.float32
    bf16 = jnp.bfloat16

    def times(lhs, rhs):
        return lax.dot_general(lhs, rhs, (((1,), (1,)), ((), ())), preferred_element_type=f32)

    normal1, weight0, _ = relay(upstream, weights[0])
    normal1 = normal1.reshape(tokens, half)

    gain_own = norm_gains[0]
    gain_mine = lax.dynamic_slice_in_dim(gain_own, core * half, half, 0)
    gain_there = shifted(lax.dynamic_slice_in_dim(gain_own, (1 - core) * half, half, 0), "section")
    gain_of = [jnp.where(core == 0, gain_mine, gain_there), jnp.where(core == 1, gain_mine, gain_there)]
    hidden_all = hidden[0].reshape(tokens, features)
    hidden_mine = columns(hidden_all, core * half, half)
    hidden_there = shifted(columns(hidden_all, (1 - core) * half, half), "section")
    hidden_of = [jnp.where(core == 0, hidden_mine, hidden_there), jnp.where(core == 1, hidden_mine, hidden_there)]
    steer_vec = columns(steering, core * half, half).astype(f32)
    layers = steer_layer.reshape(tokens)
    incoming1 = columns(upstream.reshape(tokens, features), core * half, half)

    local_sums = []
    for section in range(2):
        unsteered = hidden_of[section].astype(f32)
        moved = unsteered + steer_vec
        local_sums += [jnp.sum(unsteered * unsteered, -1), jnp.sum(moved * moved, -1)]
    local_sums.append(jnp.sum(incoming1.astype(f32) * (hidden_of[1].astype(f32) + steer_vec), -1))
    sums = lax.psum(tuple(local_sums), ("row", "section"))

    def row_total(value):
        others = [
            lax.ppermute(value, ("section", "row"), [(i, (i + d) % 4) for i in range(4)]) for d in (1, 2, 3)
        ]
        return (value + others[1]) + (others[0] + others[2])

    def finish(section, normal, incoming, inner):
        plain_sq, moved_sq = sums[2 * section], sums[2 * section + 1]
        steered = layers == section
        steered_col = steered[:, None]
        unsteered = hidden_of[section].astype(f32)
        moved = unsteered + steer_vec
        grad_float = incoming.astype(f32)
        scaled = gain_of[section].astype(f32) * normal
        chosen = jnp.where(steered_col, moved, unsteered)
        curve = row_total(jnp.sum(scaled * chosen, -1))
        norm_plain = jnp.sqrt(plain_sq + epsilon)
        norm_moved = jnp.sqrt(moved_sq + epsilon)
        rescale = norm_plain / norm_moved
        square_sum = jnp.where(
            steered, norm_plain * norm_plain * moved_sq / (norm_moved * norm_moved), plain_sq
        )
        root_mean = jnp.sqrt(square_sum / D + epsilon)
        scale = jnp.where(steered, rescale, 1.0)
        factor = scale * curve / (D * root_mean**3)
        input_grad = grad_float + scaled / root_mean[:, None] - chosen * (scale * factor)[:, None]
        radial = (inner + curve / root_mean - rescale * factor * moved_sq) / norm_moved
        tangent = rescale[:, None] * (input_grad - moved * (radial / norm_moved)[:, None])
        below = jnp.where(steered_col, tangent + unsteered * (radial / norm_plain)[:, None], input_grad)
        return below.astype(bf16), jnp.sum(jnp.where(steered_col, tangent, 0.0), 0)

    passed1, steer_part = finish(1, normal1, incoming1, sums[4])
    other = shifted(passed1, "row")
    by_row = [jnp.where(row == 0, passed1, other), jnp.where(row == 0, other, passed1)]
    there = shifted(jnp.stack(by_row), "section")
    blocks = []
    for r in range(2):
        blocks += [jnp.where(core == 0, by_row[r], there[r]), jnp.where(core == 0, there[r], by_row[r])]
    inner = row_total(jnp.sum(passed1.astype(f32) * (hidden_of[0].astype(f32) + steer_vec), -1))
    normal0 = times(blocks[0], weight0[0])
    for index in range(1, 4):
        normal0 = normal0 + times(blocks[index], weight0[index])
    passed0, steer = finish(0, normal0, passed1, inner)
    steer_part = steer_part + steer
    kept = jnp.where(core == 0, passed0, passed1)
    received = shifted(jnp.where(core == 0, passed1, passed0), "section")
    lower = jnp.where(core == 0, kept, received)
    upper = jnp.where(core == 0, received, kept)
    result = jnp.concatenate([lower, upper], 1).reshape(1, micro, row_count, features)
    steer_own = lax.psum(steer_part, "col")
    steer_other = shifted(steer_own, "section")
    steer_total = jnp.concatenate(
        [jnp.where(core == 0, steer_own, steer_other), jnp.where(core == 0, steer_other, steer_own)]
    )
    return (result, steer_total / (MICRO * ROWS))


def solution(mesh):
    placed = (
        P("section", None, ("groups", "col"), "row"),
        P(None, ("groups", "col"), "row"),
        P("section", "row", "col"),
        P("section", "row"),
        P(("groups", "row")),
        P(None, ("groups", "col")),
    )
    small = mesh.shape["row"] == 2 and mesh.shape["col"] == 4 and mesh.shape["groups"] == 2
    return jax.shard_map(
        shared_weights if small else local,
        mesh=mesh,
        in_specs=placed,
        out_specs=(P("section", None, ("groups", "col"), "row"), P(("groups", "row"))),
        check_vma=False,
    )
```

```python
import jax
import jax.numpy as jnp
from jax import lax
from jax.experimental import pallas as pl
from jax.experimental.pallas import tpu as pltpu
from jax.sharding import PartitionSpec as P

D = 8192
ROWS = 1536
MICRO = 2


epsilon = 1e-06
MESH = pl.DeviceIdType.MESH


def shifted(value, axis, steps=1):
    count = lax.axis_size(axis)
    return lax.ppermute(value, axis, [(source, (source + steps) % count) for source in range(count)])


def columns(value, start, width):
    return lax.dynamic_slice_in_dim(value, start, width, value.ndim - 1)


def after(value, earlier):
    return lax.optimization_barrier((value, earlier))[0]


def local(hidden, upstream, weights, norm_gains, steering, steer_layer):
    core = lax.axis_index("section")
    row_index = lax.axis_index("row")
    col_index = lax.axis_index("col")
    group = lax.axis_index("groups")
    row_devices = lax.axis_size("row")
    cols = lax.axis_size("col")
    groups = lax.axis_size("groups")
    micro, row_count, features = upstream.shape
    tokens = micro * row_count
    half = features // 2
    depth = weights.shape[2]
    part = depth // groups
    f32 = jnp.float32

    def own_columns(value):
        return columns(value, core * half, half)

    def per_section(mine, received):
        return jnp.where(core == 0, mine, received), jnp.where(core == 1, mine, received)

    def over_cores(value, axis):
        mine = lax.dynamic_slice_in_dim(value, core * half, half, axis)
        given = lax.dynamic_slice_in_dim(value, (1 - core) * half, half, axis)
        return per_section(mine, shifted(given, "section"))

    units = max(1, part // 128)
    step_units = max(1, units // 4)
    unit = part // units
    widths_of = {}
    for section in (1, 0):
        sizes = [step_units] * (units // step_units)
        if sum(sizes) < units:
            sizes.append(units - sum(sizes))
        widths_of[section] = [size * unit for size in sizes]
    mine = lax.dynamic_slice_in_dim(weights[0], core * half, half, 0)
    given = lax.dynamic_slice_in_dim(weights[0], (1 - core) * half, half, 0)
    lead = sum(widths_of[1][:2])
    lead_given = shifted(columns(given, group * part, lead), "section")
    first_pieces = per_section(columns(mine, group * part, lead), lead_given)
    weight_of = per_section(mine, shifted(after(given, lead_given), "section"))
    hidden_of = over_cores(hidden[0].reshape(tokens, features), 1)
    gain_of = over_cores(norm_gains[0], 0)
    steer_vec = own_columns(steering).astype(f32)
    layers = steer_layer.reshape(tokens)
    upstream_rows = upstream.reshape(tokens, features)

    earlier, sent = [], []
    pieces = {}
    for section in (1, 0):
        held = []
        start = 0
        for width in widths_of[section]:
            if start + width <= lead:
                own = first_pieces[section][:, start : start + width]
            else:
                own = columns(weight_of[section], group * part + start, width)
            if earlier:
                own = after(own, tuple(earlier))
            gathered = lax.all_gather(own, "col", axis=1, tiled=True)
            others = jnp.concatenate(
                [columns(gathered, ((col_index + step) % cols) * width, width) for step in range(1, cols)], 1
            )
            held.append((start, width, (others, shifted(others, "groups"))))
            earlier = [others] + sent[-1:]
            sent.append(held[-1][2][1])
            start += width
        pieces[section] = held

    def projected(full, section):
        def times(left, right):
            return lax.dot_general(left, right, (((1,), (1,)), ((), ())), preferred_element_type=f32)

        total = times(columns(full, col_index * depth, depth), weight_of[section])
        held = pieces[section]
        for start, width, sides in held:
            total = lax.optimization_barrier(total)
            for side, block in enumerate(sides):
                offset = ((group + side) % groups) * part + start
                left = jnp.concatenate(
                    [columns(full, ((col_index + step) % cols) * depth + offset, width) for step in range(1, cols)], 1
                )
                total = total + times(left, block)
        return total

    def all_features(own):
        if row_devices == 2:
            other = shifted(own, "row")
            both = jnp.concatenate([jnp.where(row_index == 0, own, other), jnp.where(row_index == 0, other, own)], 1)
            if own.shape[1] == features:
                return both
            there = shifted(both, "section")
            lower = jnp.where(core == 0, both, there)
            upper = jnp.where(core == 0, there, both)
            return jnp.concatenate([lower[:, :half], upper[:, :half], lower[:, half:], upper[:, half:]], 1)
        if own.shape[1] == features:
            return lax.all_gather(own, "row", axis=1, tiled=True)
        return lax.all_gather(own, ("row", "section"), axis=1, tiled=True)

    local_sums = []
    for section in range(2):
        unsteered = hidden_of[section].astype(f32)
        moved = unsteered + steer_vec
        local_sums += [jnp.sum(unsteered * unsteered, -1), jnp.sum(moved * moved, -1)]
    sums = lax.psum(tuple(local_sums), ("row", "section"))

    incoming = own_columns(upstream_rows)
    full = all_features(upstream_rows)
    steer_part = jnp.zeros((half,), f32)
    blocks = [None, None]
    for section in (1, 0):
        plain_sq, moved_sq = sums[2 * section], sums[2 * section + 1]
        steered = layers == section
        steered_col = steered[:, None]
        unsteered = hidden_of[section].astype(f32)
        moved = unsteered + steer_vec
        grad_float = incoming.astype(f32)
        scaled = gain_of[section].astype(f32) * projected(full, section)
        chosen = jnp.where(steered_col, moved, unsteered)
        curve, inner = lax.psum(
            (jnp.sum(scaled * chosen, -1), jnp.sum(grad_float * moved, -1)), ("row", "section")
        )
        norm_plain = jnp.sqrt(plain_sq + epsilon)
        norm_moved = jnp.sqrt(moved_sq + epsilon)
        rescale = norm_plain / norm_moved
        square_sum = jnp.where(
            steered, norm_plain * norm_plain * moved_sq / (norm_moved * norm_moved), plain_sq
        )
        root_mean = jnp.sqrt(square_sum / D + epsilon)
        scale = jnp.where(steered, rescale, 1.0)
        factor = scale * curve / (D * root_mean**3)
        input_grad = grad_float + scaled / root_mean[:, None] - chosen * (scale * factor)[:, None]
        radial = (inner + curve / root_mean - rescale * factor * moved_sq) / norm_moved
        tangent = rescale[:, None] * (input_grad - moved * (radial / norm_moved)[:, None])
        below = jnp.where(steered_col, tangent + unsteered * (radial / norm_plain)[:, None], input_grad)
        passed = below.astype(jnp.bfloat16)
        blocks[section] = passed
        steer_part = steer_part + jnp.sum(jnp.where(steered_col, tangent, 0.0), 0)
        if section == 1:
            incoming = passed
            full = all_features(passed)
    kept = jnp.where(core == 0, blocks[0], blocks[1])
    received = shifted(jnp.where(core == 0, blocks[1], blocks[0]), "section")
    lower = jnp.where(core == 0, kept, received)
    upper = jnp.where(core == 0, received, kept)
    result = jnp.concatenate([lower, upper], 1).reshape(1, micro, row_count, features)
    steer_own = lax.psum(steer_part, "col")
    steer_other = shifted(steer_own, "section")
    steer_total = jnp.concatenate(
        [jnp.where(core == 0, steer_own, steer_other), jnp.where(core == 0, steer_other, steer_own)]
    )
    return (result, steer_total / (MICRO * ROWS))


CHUNKS = 3


def chunk_rows(part):
    widths = [part // 2, part // 4, part // 4]
    return [(0, widths[0]), (widths[0], widths[1]), (widths[0] + widths[1], widths[2])]


def relay_kernel(
    u, w, hidden, gains, steer, lay, res, steer_out, wg, q, xc, w1, partial, total, got, hv, gain_of, stat, curve, coef,
    steer_acc, steer_all, own_sem, w1_sem, half_send, x1_send, x1_recv, a_send, a_recv, a_local, x2_send, x2_recv,
    c_send, c_recv, f_send, f_recv, wr_send, wr_recv, wl_send, wl_recv, y_send, y_recv, r_send, r_recv, l_send, l_recv,
    hid_send, hid_recv, hid_local, gain_sem, gain_send, stat_send, stat_recv, curve_send, curve_recv, u_sem, p_send,
    p_recv, tile_sem, out_sem, out_send, s_send, s_recv, s_local, t_sem, t_send
):
    core, row, col, group = (lax.axis_index(name) for name in ("section", "row", "col", "groups"))
    micro, row_count, features = u.shape
    half = features // 2
    part = half // 2
    quarter = row_count // 4
    cols = 4
    last = cols - 1
    f32 = jnp.float32
    chunks = chunk_rows(part)
    from_left_slot, from_right_slot = (0, 1, 2), (0, 3, 4)
    my_half = pl.ds(pl.multiple_of(core * half, half), half)
    other_half = pl.ds(pl.multiple_of((1 - core) * half, half), half)
    my_block = row * 2 + core

    barrier = pltpu.get_barrier_semaphore()
    peers = [{"col": (col + step) % cols} for step in range(1, cols)]
    peers += [{"row": 1 - row}, {"groups": 1 - group}, {"section": 1 - core}, {"row": 1 - row, "section": 1 - core}]
    for peer in peers:
        pl.semaphore_signal(barrier, inc=1, device_id=peer, device_id_type=MESH)
    pl.semaphore_wait(barrier, len(peers))

    late = []

    class Send:
        def __init__(self, src, dst, send, recv, device, when=None):
            self.copy = pltpu.make_async_remote_copy(
                src_ref=src, dst_ref=dst, send_sem=send, recv_sem=recv, device_id=device, device_id_type=MESH
            )
            self.when = when
            self.waited = False
            late.append(self)
            self.guarded(self.copy.start)

        def guarded(self, action):
            if self.when is None:
                action()
            else:
                pl.when(self.when)(lambda: action())

        def wait_send(self):
            if not self.waited:
                self.waited = True
                self.guarded(self.copy.wait_send)

    def arrived(ref, sem, when=None):
        copy = pltpu.make_async_remote_copy(
            src_ref=ref, dst_ref=ref, send_sem=sem, recv_sem=sem, device_id={"section": 1 - core}, device_id_type=MESH
        )
        if when is None:
            copy.wait_recv()
        else:
            pl.when(when)(lambda: copy.wait_recv())

    for order in range(2):
        h = (group + order) % 2
        mine, there = pl.ds(h * part, part), pl.ds(half + h * part, part)

        @pl.when(core == 0)
        def _():
            pltpu.make_async_remote_copy(
                src_ref=w.at[there], dst_ref=wg.at[col, mine], send_sem=half_send.at[order], recv_sem=own_sem.at[order],
                device_id={"section": 1 - core}, device_id_type=MESH,
            ).start()
            pltpu.make_async_copy(w.at[mine], wg.at[col, mine], own_sem.at[order]).start()

        @pl.when(core == 1)
        def _():
            pltpu.make_async_remote_copy(
                src_ref=w.at[mine], dst_ref=w1.at[mine], send_sem=half_send.at[order], recv_sem=w1_sem.at[order],
                device_id={"section": 1 - core}, device_id_type=MESH,
            ).start()
            pltpu.make_async_copy(w.at[there], w1.at[mine], w1_sem.at[order]).start()

    def wait_own(order):
        mine = pl.ds(((group + order) % 2) * part, part)
        pltpu.make_async_copy(w.at[mine], wg.at[col, mine], own_sem.at[order]).wait()

    def wait_w1(order):
        mine = pl.ds(((group + order) % 2) * part, part)
        pltpu.make_async_copy(w.at[mine], w1.at[mine], w1_sem.at[order]).wait()

    my_rows = pl.ds((row * 2 + core) * quarter, quarter)
    x1 = [
        Send(u.at[m, pl.ds(((1 - row) * 2 + core) * quarter, quarter)], q.at[m], x1_send.at[m], x1_recv.at[m], {"row": 1 - row})
        for m in range(micro)
    ]

    def columns_of(index):
        return pl.ds(pl.multiple_of((index % 2) * half, half), half)

    def to_cols(m, from_own):
        for step in range(cols):
            there = (col + step) % cols
            here = (there // 2) == row
            src = u.at[m, my_rows, columns_of(there)] if from_own else q.at[m, :, columns_of(there)]
            when = here if from_own else jnp.logical_not(here)
            dst = xc.at[m, col, my_rows]
            if step == 0:
                pl.when(when)(lambda: pltpu.make_async_copy(src, dst, a_local.at[m]).start())
            else:
                Send(src, dst, a_send.at[m, step, int(from_own)], a_recv.at[m, step], {"col": there}, when)

    z_sent = []

    def z_step(sends):
        z_sent.append(sends)
        if len(z_sent) > 2:
            for send in z_sent[-3]:
                send.wait_send()

    def w_rows(k):
        return pl.ds(pl.multiple_of(group * part + chunks[k][0], 128), chunks[k][1])

    def w_hop(hop, k):
        from_right, from_left = jnp.maximum(col - hop + 1, 0), jnp.minimum(col + hop - 1, last)
        return [
            Send(
                wg.at[from_right, w_rows(k)], wg.at[from_right, w_rows(k)], wr_send.at[hop - 1, k], wr_recv.at[hop - 1, k],
                {"col": jnp.minimum(col + 1, last)}, (col < last) & (col - hop + 1 >= 0),
            ),
            Send(
                wg.at[from_left, w_rows(k)], wg.at[from_left, w_rows(k)], wl_send.at[hop - 1, k], wl_recv.at[hop - 1, k],
                {"col": jnp.maximum(col - 1, 0)}, (col > 0) & (col + hop - 1 <= last),
            ),
        ]

    def w_arrived(hop, k):
        arrived(wg.at[jnp.maximum(col - hop, 0), w_rows(k)], wr_recv.at[hop - 1, k], col - hop >= 0)
        arrived(wg.at[jnp.minimum(col + hop, last), w_rows(k)], wl_recv.at[hop - 1, k], col + hop <= last)

    sources = [
        jnp.where(col == 0, 1, jnp.maximum(col - 1, 0)),
        (col + 2) % cols,
        jnp.where(col == 0, last, (col + 1) % cols),
    ]
    y_sent = []

    def y_swap(slot, k):
        if len(y_sent) > 1:
            y_sent[-2].wait_send()
        ref = wg.at[sources[slot], w_rows(k)]
        y_sent.append(Send(ref, ref, y_send.at[slot, k], y_recv.at[slot, k], {"groups": 1 - group}))

    def y_arrived(slot, k):
        rows = pl.ds(pl.multiple_of((1 - group) * part + chunks[k][0], 128), chunks[k][1])
        arrived(wg.at[sources[slot], rows], y_recv.at[slot, k])

    to_cols(0, True)
    wait_own(0)
    z_step(w_hop(1, 0))
    arrived(q.at[0], x1_recv.at[0])
    to_cols(0, False)
    to_cols(1, True)
    arrived(q.at[1], x1_recv.at[1])
    to_cols(1, False)

    def quarter_rows(row_at, core_at):
        return pl.ds((row_at * 2 + core_at) * quarter, quarter)

    token_sends = [[], []]

    def gather(m):
        for step in range(cols):
            source = (col - step) % cols
            ref = xc.at[m, source, my_rows]
            if step == 0:
                pltpu.make_async_copy(ref, ref, a_local.at[m]).wait()
            else:
                arrived(ref, a_recv.at[m, step])
            token_sends[m].append(Send(ref, ref, x2_send.at[m, step], x2_recv.at[m, step], {"row": 1 - row}))
            token_sends[m].append(Send(ref, ref, c_send.at[m, step], c_recv.at[m, step], {"section": 1 - core}))

    def gather_rest(m):
        for step in range(cols):
            ref = xc.at[m, (col - step) % cols, quarter_rows(1 - row, core)]
            arrived(ref, x2_recv.at[m, step])
            token_sends[m].append(Send(ref, ref, f_send.at[m, step], f_recv.at[m, step], {"section": 1 - core}))
        for step in range(cols):
            arrived(xc.at[m, (col - step) % cols, quarter_rows(row, 1 - core)], c_recv.at[m, step])
            arrived(xc.at[m, (col - step) % cols, quarter_rows(1 - row, 1 - core)], f_recv.at[m, step])

    tile = 512

    def multiply(m):
        @pl.loop(0, cols)
        def _(index):
            step = jnp.where(col == last, last - index, (index + 1) % cols)
            source = (col - step + cols) % cols

            @pl.loop(0, half // tile)
            def _(block):
                at = pl.ds(pl.multiple_of(block * tile, tile), tile)
                value = lax.dot_general(
                    xc[m, source], w1[at, :], (((1,), (1,)), ((), ())), preferred_element_type=f32
                )

                @pl.when(step == 0)
                def _():
                    total[m, :, at] = value

                @pl.when(step > 0)
                def _():
                    partial[m, jnp.maximum(step - 1, 0), :, at] = value.astype(jnp.bfloat16)

    def add(dst, src, when):
        @pl.when(when)
        def _():
            @pl.loop(0, row_count // 32)
            def _(block):
                at = pl.ds(pl.multiple_of(block * 32, 32), 32)
                dst[at, :] = (dst[at, :].astype(f32) + src[at, :].astype(f32)).astype(dst.dtype)

    sum_sends = [[], []]

    def sums_step(m, tau):
        right, left = (col <= tau) & (col < last), (last - col <= tau) & (col > 0)
        to_right, to_left = partial.at[m, tau], partial.at[m, 2 - tau]
        if tau > 0:
            arrived(got.at[m, from_left_slot[tau - 1]], r_recv.at[m, tau - 1], (col >= 1) & (col <= tau))
            add(to_right, got.at[m, from_left_slot[tau - 1]], right & (col >= 1))
        sends = [
            Send(to_right, got.at[m, from_left_slot[tau]], r_send.at[m, tau], r_recv.at[m, tau], {"col": jnp.minimum(col + 1, last)}, right)
        ]
        if tau > 0:
            arrived(got.at[m, from_right_slot[tau - 1]], l_recv.at[m, tau - 1], (col < last) & (last - col <= tau))
            add(to_left, got.at[m, from_right_slot[tau - 1]], left & (col < last))
        sends.append(
            Send(to_left, got.at[m, from_right_slot[tau]], l_send.at[m, tau], l_recv.at[m, tau], {"col": jnp.maximum(col - 1, 0)}, left)
        )
        sum_sends[m] += sends
        return sends

    def finish(m):
        arrived(got.at[m, from_left_slot[last - 1]], r_recv.at[m, last - 1], col >= 1)
        add(total.at[m], got.at[m, from_left_slot[last - 1]], col >= 1)
        arrived(got.at[m, from_right_slot[last - 1]], l_recv.at[m, last - 1], col < last)
        add(total.at[m], got.at[m, from_right_slot[last - 1]], col < last)

    def hidden_copies():
        for section in range(2):
            @pl.when(core == section)
            def _():
                for m in range(micro):
                    pltpu.make_async_copy(hidden.at[m, :, my_half], hv.at[section, m], hid_local.at[m]).start()
                    pltpu.make_async_remote_copy(
                        src_ref=hidden.at[m, :, other_half], dst_ref=hv.at[section, m], send_sem=hid_send.at[m],
                        recv_sem=hid_recv.at[m], device_id={"section": 1 - core}, device_id_type=MESH,
                    ).start()
                pltpu.make_async_copy(gains.at[:, my_half], gain_of.at[section], gain_sem.at[0]).start()
                pltpu.make_async_remote_copy(
                    src_ref=gains.at[:, other_half], dst_ref=gain_of.at[section], send_sem=gain_send,
                    recv_sem=gain_sem.at[1], device_id={"section": 1 - core}, device_id_type=MESH,
                ).start()

    def hidden_wait():
        for m in range(micro):
            pltpu.make_async_copy(hidden.at[m, :, my_half], hv.at[0, m], hid_local.at[m]).wait()
            arrived(hv.at[0, m], hid_recv.at[m])
        pltpu.make_async_copy(gains.at[:, my_half], gain_of.at[0], gain_sem.at[0]).wait()
        arrived(gain_of.at[0], gain_sem.at[1])

    def hidden_sent():
        for m in range(micro):
            pltpu.make_async_remote_copy(
                src_ref=hidden.at[m, :, other_half], dst_ref=hv.at[0, m], send_sem=hid_send.at[m],
                recv_sem=hid_recv.at[m], device_id={"section": 1 - core}, device_id_type=MESH,
            ).wait_send()
        pltpu.make_async_remote_copy(
            src_ref=gains.at[:, other_half], dst_ref=gain_of.at[0], send_sem=gain_send, recv_sem=gain_sem.at[1],
            device_id={"section": 1 - core}, device_id_type=MESH,
        ).wait_send()

    quad = [{"row": 1 - row}, {"section": 1 - core}, {"row": 1 - row, "section": 1 - core}]
    block_rows, block_cols = 16, 512
    lane = lax.broadcasted_iota(jnp.int32, (block_rows, 128), 1)

    def spread(values):
        result = jnp.zeros((block_rows, 128), f32)
        for index, value in enumerate(values):
            result = jnp.where(lane == index, value, result)
        return result

    def row_blocks(body):
        @pl.loop(0, row_count // block_rows)
        def _(index):
            body(pl.ds(pl.multiple_of(index * block_rows, block_rows), block_rows))

    def column_blocks():
        for index in range(half // block_cols):
            here = pl.ds(index * block_cols, block_cols)
            there = pl.ds(pl.multiple_of(core * half + index * block_cols, block_cols), block_cols)
            yield here, steer[0:1, there]

    def row_sum(value):
        return jnp.sum(value, -1, keepdims=True)

    def statistics(m):
        def body(at):
            sums = [jnp.zeros((block_rows, block_cols), f32) for _ in range(4)]
            for here, vector in column_blocks():
                for section in range(2):
                    plain = hv[section, m, at, here].astype(f32)
                    moved = plain + vector
                    sums[2 * section] += plain * plain
                    sums[2 * section + 1] += moved * moved
            stat[m, 0, at, :] = spread([row_sum(value) for value in sums])

        row_blocks(body)
        for index, peer in enumerate(quad):
            Send(stat.at[m, 0], stat.at[m, index + 1], stat_send.at[m, index], stat_recv.at[m, index], peer)

    def statistics_wait(m):
        for index in range(3):
            arrived(stat.at[m, index + 1], stat_recv.at[m, index])

    def load_upstream(m):
        pltpu.make_async_copy(u.at[m, :, my_half], got.at[m, 0], u_sem.at[m]).start()

    curve_sends = {}

    def curvature(section, m):
        incoming = got.at[m, 0] if section == 1 else xc.at[m, my_block]
        for send in curve_sends.get(m, []):
            send.wait_send()

        def body(at):
            steered = lay[m, at, 0:1] == float(section)
            curved = jnp.zeros((block_rows, block_cols), f32)
            inner = jnp.zeros((block_rows, block_cols), f32)
            for here, vector in column_blocks():
                plain = hv[section, m, at, here].astype(f32)
                moved = plain + vector
                scaled = gain_of[section, 0:1, here] * total[m, at, here]
                curved += scaled * jnp.where(steered, moved, plain)
                inner += incoming[at, here].astype(f32) * moved
            curve[m, 0, at, :] = spread([row_sum(curved), row_sum(inner)])

        row_blocks(body)
        curve_sends[m] = [
            Send(
                curve.at[m, 0], curve.at[m, index + 1], curve_send.at[section, m, index],
                curve_recv.at[section, m, index], peer,
            )
            for index, peer in enumerate(quad)
        ]

    def gradient(section, m, out):
        for index in range(3):
            arrived(curve.at[m, index + 1], curve_recv.at[section, m, index])
        if section == 1:
            statistics_wait(m)
        span = 128

        @pl.loop(0, row_count // span)
        def _(index):
            at = pl.ds(pl.multiple_of(index * span, span), span)
            both = (curve[m, 0, at, :] + curve[m, 1, at, :]) + (curve[m, 2, at, :] + curve[m, 3, at, :])
            sums = (stat[m, 0, at, :] + stat[m, 1, at, :]) + (stat[m, 2, at, :] + stat[m, 3, at, :])
            curved, inner = both[:, 0:1], both[:, 1:2]
            plain_sq, moved_sq = sums[:, 2 * section : 2 * section + 1], sums[:, 2 * section + 1 : 2 * section + 2]
            steered = lay[m, at, 0:1] == float(section)
            norm_plain = jnp.sqrt(plain_sq + epsilon)
            norm_moved = jnp.sqrt(moved_sq + epsilon)
            rescale = norm_plain / norm_moved
            square_sum = jnp.where(
                steered, norm_plain * norm_plain * moved_sq / (norm_moved * norm_moved), plain_sq
            )
            root_mean = jnp.sqrt(square_sum / D + epsilon)
            scale = jnp.where(steered, rescale, 1.0)
            factor = scale * curved / (D * (root_mean * root_mean * root_mean))
            radial = (inner + curved / root_mean - rescale * factor * moved_sq) / norm_moved
            wide = lax.broadcasted_iota(jnp.int32, (span, 128), 1)
            result = jnp.zeros((span, 128), f32)
            terms = (1.0 / root_mean, scale * factor, rescale, radial / norm_moved, radial / norm_plain)
            for place, value in enumerate(terms):
                result = jnp.where(wide == place, value, result)
            coef[at, :] = result

        incoming = got.at[m, 0] if section == 1 else xc.at[m, my_block]

        def body(at):
            steered = lay[m, at, 0:1] == float(section)
            inverse, pull, rescale, along, back = [coef[at, place : place + 1] for place in range(5)]
            for here, vector in column_blocks():
                plain = hv[section, m, at, here].astype(f32)
                moved = plain + vector
                scaled = gain_of[section, 0:1, here] * total[m, at, here]
                grad = incoming[at, here].astype(f32) + scaled * inverse - jnp.where(steered, moved, plain) * pull
                tangent = rescale * (grad - moved * along)
                out[at, here] = jnp.where(steered, tangent + plain * back, grad).astype(jnp.bfloat16)
                kept = jnp.where(steered, tangent, 0.0)
                steer_acc[:, here] += kept[:8] + kept[8:]

        row_blocks(body)
        @pl.when(core == section)
        def _():
            pltpu.make_async_copy(out, res.at[m, :, my_half], out_sem.at[0, m]).start()

        @pl.when(core != section)
        def _():
            pltpu.make_async_remote_copy(
                src_ref=out, dst_ref=res.at[m, :, my_half], send_sem=out_send.at[m], recv_sem=out_sem.at[1, m],
                device_id={"section": 1 - core}, device_id_type=MESH,
            ).start()

    def out_wait(section, m):
        pltpu.make_async_remote_copy(
            src_ref=partial.at[m, 0], dst_ref=res.at[m, :, my_half], send_sem=out_send.at[m], recv_sem=out_sem.at[1, m],
            device_id={"section": 1 - core}, device_id_type=MESH,
        ).wait_send()

    def pass_down(m):
        ref = xc.at[m, my_block]
        Send(ref, ref, p_send.at[m, 0], p_recv.at[m, 0], {"row": 1 - row})
        Send(ref, ref, p_send.at[m, 1], p_recv.at[m, 1], {"section": 1 - core})

    def pass_on(m):
        ref = xc.at[m, (1 - row) * 2 + core]
        arrived(ref, p_recv.at[m, 0])
        Send(ref, ref, p_send.at[m, 2], p_recv.at[m, 2], {"section": 1 - core})

    def pass_wait(m):
        arrived(xc.at[m, row * 2 + 1 - core], p_recv.at[m, 1])
        arrived(xc.at[m, (1 - row) * 2 + 1 - core], p_recv.at[m, 2])

    def section_one(m):
        finish(m)
        for send in token_sends[m]:
            send.wait_send()
        pltpu.make_async_copy(u.at[m, :, my_half], got.at[m, 0], u_sem.at[m]).wait()
        curvature(1, m)
        gradient(1, m, xc.at[m, my_block])
        pass_down(m)

    width = 256
    per_half = (part - chunks[-1][1]) // width
    own_tiles = half // width
    tail_tiles = chunks[-1][1] // width

    def early_tile(index):
        rest = jnp.maximum(index - own_tiles, 0)
        source = (col + 1 + rest // (2 * per_half)) % cols
        inside = rest % (2 * per_half)
        start = (inside // per_half) * part + (inside % per_half) * width
        own = index < own_tiles
        return jnp.where(own, col, source), jnp.where(own, index * width, start)

    def tail_tile(index):
        source = (col + 1 + index // (2 * tail_tiles)) % cols
        inside = index % (2 * tail_tiles)
        return source, (inside // tail_tiles) * part + chunks[-1][0] + (inside % tail_tiles) * width

    def products(batches, count, tile_of, first):
        def load(index):
            source, start = tile_of(index)
            slot = index % 2
            return pltpu.make_async_copy(
                wg.at[source, pl.ds(pl.multiple_of(start, width), width)],
                w1.at[pl.ds(pl.multiple_of(slot * width, width), width)],
                tile_sem.at[slot],
            )

        load(jnp.int32(0)).start()

        @pl.loop(0, count)
        def _(index):
            pl.when(index + 1 < count)(lambda: load(index + 1).start())
            load(index).wait()
            source, start = tile_of(index)
            rows = pl.ds(pl.multiple_of((index % 2) * width, width), width)
            at = pl.ds(pl.multiple_of(start, width), width)
            for m in batches:
                value = lax.dot_general(
                    xc[m, source], w1[rows, :], (((1,), (1,)), ((), ())), preferred_element_type=f32
                )
                if first:
                    @pl.when(index < own_tiles)
                    def _():
                        total[m, :, at] = value

                    @pl.when(index >= own_tiles)
                    def _():
                        total[m, :, at] += value
                else:
                    total[m, :, at] += value

    early_count = own_tiles + 6 * per_half
    steer_acc[...] = jnp.zeros_like(steer_acc)

    hidden_copies()
    gather(0)
    z_step(w_hop(1, 1))
    hidden_wait()
    statistics(0)
    statistics(1)
    gather_rest(0)
    w_arrived(1, 0)
    y_swap(0, 0)
    wait_w1(0)
    wait_w1(1)
    multiply(0)
    z_step(sums_step(0, 0) + w_hop(2, 0))
    gather(1)
    w_arrived(1, 1)
    y_swap(0, 1)
    z_step(sums_step(0, 1))
    load_upstream(0)
    gather_rest(1)
    multiply(1)
    w_arrived(2, 0)
    z_step(w_hop(3, 0))
    y_swap(1, 0)
    z_step(sums_step(1, 0) + w_hop(2, 1))
    z_step(sums_step(0, 2))
    w_arrived(3, 0)
    y_swap(2, 0)
    z_step(sums_step(1, 1))
    load_upstream(1)
    w_arrived(2, 1)
    z_step(w_hop(3, 1))
    y_swap(1, 1)
    section_one(0)
    z_step(sums_step(1, 2) + w_hop(1, 2))
    w_arrived(3, 1)
    y_swap(2, 1)
    pass_on(0)
    w_arrived(1, 2)
    z_step(w_hop(2, 2))
    y_swap(0, 2)
    section_one(1)
    w_arrived(2, 2)
    z_step(w_hop(3, 2))
    y_swap(1, 2)
    wait_own(1)
    for k in range(CHUNKS - 1):
        for slot in range(3):
            y_arrived(slot, k)
    pass_wait(0)
    products([0], early_count, early_tile, True)
    pass_on(1)
    w_arrived(3, 2)
    y_swap(2, 2)
    pass_wait(1)
    products([1], early_count, early_tile, True)
    for slot in range(3):
        y_arrived(slot, CHUNKS - 1)
    products([0, 1], 6 * tail_tiles, tail_tile, False)
    for m in range(micro):
        for send in sum_sends[m]:
            send.wait_send()
    for m in range(micro):
        pl.when(core == 0)(lambda: out_wait(1, m))
        curvature(0, m)
    for m in range(micro):
        gradient(0, m, partial.at[m, 0])

    own_copy = pltpu.make_async_copy(steer_acc, steer_all.at[col], s_local)
    own_copy.start()
    for step in range(1, cols):
        there = (col + step) % cols
        Send(steer_acc, steer_all.at[col], s_send.at[step], s_recv.at[step], {"col": there})
    own_copy.wait()
    for step in range(1, cols):
        arrived(steer_all.at[(col - step) % cols], s_recv.at[step])
    for send in late:
        send.wait_send()
    steer_acc[...] = (steer_all[0] + steer_all[1]) + (steer_all[2] + steer_all[3])
    final = pltpu.make_async_copy(steer_acc, steer_out.at[core], t_sem.at[0])
    final.start()
    give = pltpu.make_async_remote_copy(
        src_ref=steer_acc, dst_ref=steer_out.at[core], send_sem=t_send, recv_sem=t_sem.at[1],
        device_id={"section": 1 - core}, device_id_type=MESH,
    )
    give.start()
    final.wait()
    give.wait()

    for order in range(2):
        pltpu.make_async_remote_copy(
            src_ref=w.at[pl.ds(0, part)], dst_ref=wg.at[col, pl.ds(0, part)], send_sem=half_send.at[order],
            recv_sem=own_sem.at[order], device_id={"section": 1 - core}, device_id_type=MESH,
        ).wait_send()
    hidden_sent()
    for m in range(micro):
        pltpu.make_async_copy(partial.at[m, 0], res.at[m, :, my_half], out_sem.at[0, m]).wait()
        arrived(res.at[m, :, other_half], out_sem.at[1, m])
        pl.when(core == 1)(lambda: out_wait(0, m))


def relay(u, w, hidden, gains, steer, lay):
    micro, row_count, features = u.shape
    half = features // 2
    dma = pltpu.SemaphoreType.DMA
    bf16, f32 = jnp.bfloat16, jnp.float32
    in_vmem = pl.BlockSpec(memory_space=pltpu.VMEM)
    anywhere = pl.BlockSpec(memory_space=pl.ANY)
    return pl.pallas_call(
        relay_kernel,
        out_shape=(
            jax.ShapeDtypeStruct((micro, row_count, features), bf16),
            jax.ShapeDtypeStruct((2, 8, half), f32),
            jax.ShapeDtypeStruct((4, half, half), bf16),
            jax.ShapeDtypeStruct((micro, row_count // 4, features), bf16),
        ),
        in_specs=[anywhere, anywhere, anywhere, anywhere, in_vmem, in_vmem],
        out_specs=(anywhere,) * 4,
        scratch_shapes=[
            pltpu.VMEM((micro, 4, row_count, half), bf16),
            pltpu.VMEM((half, half), bf16),
            pltpu.VMEM((micro, 3, row_count, half), bf16),
            pltpu.VMEM((micro, row_count, half), f32),
            pltpu.VMEM((micro, 5, row_count, half), bf16),
            pltpu.VMEM((2, micro, row_count, half), bf16),
            pltpu.VMEM((2, 8, half), f32),
            pltpu.VMEM((micro, 4, row_count, 128), f32),
            pltpu.VMEM((micro, 4, row_count, 128), f32),
            pltpu.VMEM((row_count, 128), f32),
            pltpu.VMEM((8, half), f32),
            pltpu.VMEM((4, 8, half), f32),
            dma((2,)), dma((2,)), dma((2,)),
            dma((2,)), dma((2,)),
            dma((2, 4, 2)), dma((2, 4)), dma((2,)),
            dma((2, 4)), dma((2, 4)), dma((2, 4)), dma((2, 4)), dma((2, 4)), dma((2, 4)),
            dma((3, CHUNKS)), dma((3, CHUNKS)), dma((3, CHUNKS)), dma((3, CHUNKS)),
            dma((3, CHUNKS)), dma((3, CHUNKS)),
            dma((2, 3)), dma((2, 3)), dma((2, 3)), dma((2, 3)),
            dma((2,)), dma((2,)), dma((2,)), dma((2,)), dma,
            dma((2, 3)), dma((2, 3)),
            dma((2, 2, 3)), dma((2, 2, 3)),
            dma((2,)),
            dma((2, 3)), dma((2, 3)),
            dma((2,)),
            dma((2, 2)), dma((2,)),
            dma((4,)), dma((4,)), dma, dma((2,)), dma,
        ],
        compiler_params=pltpu.CompilerParams(
            collective_id=0, has_side_effects=True, vmem_limit_bytes=63 * 1024 * 1024
        ),
        cost_estimate=pl.CostEstimate(
            flops=4 * micro * 4 * row_count * half * half, bytes_accessed=150 * 1024 * 1024, transcendentals=0
        ),
        name="relay",
    )(u, w, hidden, gains, steer, lay)


def shared_weights(hidden, upstream, weights, norm_gains, steering, steer_layer):
    features = upstream.shape[2]
    f32 = jnp.float32
    gains = jnp.broadcast_to(norm_gains[0].astype(f32), (8, features))
    steer = jnp.broadcast_to(steering.astype(f32), (8, features))
    lay = jnp.broadcast_to(steer_layer.astype(f32)[:, :, None], steer_layer.shape + (128,))
    result, steer_parts, _, _ = relay(upstream, weights[0], hidden[0], gains, steer, lay)
    steer_total = jnp.sum(steer_parts, 1).reshape(features)
    return (result[None], steer_total / (MICRO * ROWS))


def solution(mesh):
    placed = (
        P("section", None, ("groups", "col"), "row"),
        P(None, ("groups", "col"), "row"),
        P("section", "row", "col"),
        P("section", "row"),
        P(("groups", "row")),
        P(None, ("groups", "col")),
    )
    small = mesh.shape["row"] == 2 and mesh.shape["col"] == 4 and mesh.shape["groups"] == 2
    return jax.shard_map(
        shared_weights if small else local,
        mesh=mesh,
        in_specs=placed,
        out_specs=(P("section", None, ("groups", "col"), "row"), P(("groups", "row"))),
        check_vma=False,
    )
```

```python
import jax
import jax.numpy as jnp
from jax import lax
from jax.experimental import pallas as pl
from jax.experimental.pallas import tpu as pltpu
from jax.sharding import PartitionSpec as P

D = 8192
ROWS = 1536
MICRO = 2


epsilon = 1e-06
MESH = pl.DeviceIdType.MESH


def shifted(value, axis, steps=1):
    count = lax.axis_size(axis)
    return lax.ppermute(value, axis, [(source, (source + steps) % count) for source in range(count)])


def columns(value, start, width):
    return lax.dynamic_slice_in_dim(value, start, width, value.ndim - 1)


def after(value, earlier):
    return lax.optimization_barrier((value, earlier))[0]


def local(hidden, upstream, weights, norm_gains, steering, steer_layer):
    core = lax.axis_index("section")
    row_index = lax.axis_index("row")
    col_index = lax.axis_index("col")
    group = lax.axis_index("groups")
    row_devices = lax.axis_size("row")
    cols = lax.axis_size("col")
    groups = lax.axis_size("groups")
    micro, row_count, features = upstream.shape
    tokens = micro * row_count
    half = features // 2
    depth = weights.shape[2]
    part = depth // groups
    f32 = jnp.float32

    def own_columns(value):
        return columns(value, core * half, half)

    def per_section(mine, received):
        return jnp.where(core == 0, mine, received), jnp.where(core == 1, mine, received)

    def over_cores(value, axis):
        mine = lax.dynamic_slice_in_dim(value, core * half, half, axis)
        given = lax.dynamic_slice_in_dim(value, (1 - core) * half, half, axis)
        return per_section(mine, shifted(given, "section"))

    units = max(1, part // 128)
    step_units = max(1, units // 4)
    unit = part // units
    widths_of = {}
    for section in (1, 0):
        sizes = [step_units] * (units // step_units)
        if sum(sizes) < units:
            sizes.append(units - sum(sizes))
        widths_of[section] = [size * unit for size in sizes]
    mine = lax.dynamic_slice_in_dim(weights[0], core * half, half, 0)
    given = lax.dynamic_slice_in_dim(weights[0], (1 - core) * half, half, 0)
    lead = sum(widths_of[1][:2])
    lead_given = shifted(columns(given, group * part, lead), "section")
    first_pieces = per_section(columns(mine, group * part, lead), lead_given)
    weight_of = per_section(mine, shifted(after(given, lead_given), "section"))
    hidden_of = over_cores(hidden[0].reshape(tokens, features), 1)
    gain_of = over_cores(norm_gains[0], 0)
    steer_vec = own_columns(steering).astype(f32)
    layers = steer_layer.reshape(tokens)
    upstream_rows = upstream.reshape(tokens, features)

    earlier, sent = [], []
    pieces = {}
    for section in (1, 0):
        held = []
        start = 0
        for width in widths_of[section]:
            if start + width <= lead:
                own = first_pieces[section][:, start : start + width]
            else:
                own = columns(weight_of[section], group * part + start, width)
            if earlier:
                own = after(own, tuple(earlier))
            gathered = lax.all_gather(own, "col", axis=1, tiled=True)
            others = jnp.concatenate(
                [columns(gathered, ((col_index + step) % cols) * width, width) for step in range(1, cols)], 1
            )
            held.append((start, width, (others, shifted(others, "groups"))))
            earlier = [others] + sent[-1:]
            sent.append(held[-1][2][1])
            start += width
        pieces[section] = held

    def projected(full, section):
        def times(left, right):
            return lax.dot_general(left, right, (((1,), (1,)), ((), ())), preferred_element_type=f32)

        total = times(columns(full, col_index * depth, depth), weight_of[section])
        held = pieces[section]
        for start, width, sides in held:
            total = lax.optimization_barrier(total)
            for side, block in enumerate(sides):
                offset = ((group + side) % groups) * part + start
                left = jnp.concatenate(
                    [columns(full, ((col_index + step) % cols) * depth + offset, width) for step in range(1, cols)], 1
                )
                total = total + times(left, block)
        return total

    def all_features(own):
        if row_devices == 2:
            other = shifted(own, "row")
            both = jnp.concatenate([jnp.where(row_index == 0, own, other), jnp.where(row_index == 0, other, own)], 1)
            if own.shape[1] == features:
                return both
            there = shifted(both, "section")
            lower = jnp.where(core == 0, both, there)
            upper = jnp.where(core == 0, there, both)
            return jnp.concatenate([lower[:, :half], upper[:, :half], lower[:, half:], upper[:, half:]], 1)
        if own.shape[1] == features:
            return lax.all_gather(own, "row", axis=1, tiled=True)
        return lax.all_gather(own, ("row", "section"), axis=1, tiled=True)

    local_sums = []
    for section in range(2):
        unsteered = hidden_of[section].astype(f32)
        moved = unsteered + steer_vec
        local_sums += [jnp.sum(unsteered * unsteered, -1), jnp.sum(moved * moved, -1)]
    sums = lax.psum(tuple(local_sums), ("row", "section"))

    incoming = own_columns(upstream_rows)
    full = all_features(upstream_rows)
    steer_part = jnp.zeros((half,), f32)
    blocks = [None, None]
    for section in (1, 0):
        plain_sq, moved_sq = sums[2 * section], sums[2 * section + 1]
        steered = layers == section
        steered_col = steered[:, None]
        unsteered = hidden_of[section].astype(f32)
        moved = unsteered + steer_vec
        grad_float = incoming.astype(f32)
        scaled = gain_of[section].astype(f32) * projected(full, section)
        chosen = jnp.where(steered_col, moved, unsteered)
        curve, inner = lax.psum(
            (jnp.sum(scaled * chosen, -1), jnp.sum(grad_float * moved, -1)), ("row", "section")
        )
        norm_plain = jnp.sqrt(plain_sq + epsilon)
        norm_moved = jnp.sqrt(moved_sq + epsilon)
        rescale = norm_plain / norm_moved
        square_sum = jnp.where(
            steered, norm_plain * norm_plain * moved_sq / (norm_moved * norm_moved), plain_sq
        )
        root_mean = jnp.sqrt(square_sum / D + epsilon)
        scale = jnp.where(steered, rescale, 1.0)
        factor = scale * curve / (D * root_mean**3)
        input_grad = grad_float + scaled / root_mean[:, None] - chosen * (scale * factor)[:, None]
        radial = (inner + curve / root_mean - rescale * factor * moved_sq) / norm_moved
        tangent = rescale[:, None] * (input_grad - moved * (radial / norm_moved)[:, None])
        below = jnp.where(steered_col, tangent + unsteered * (radial / norm_plain)[:, None], input_grad)
        passed = below.astype(jnp.bfloat16)
        blocks[section] = passed
        steer_part = steer_part + jnp.sum(jnp.where(steered_col, tangent, 0.0), 0)
        if section == 1:
            incoming = passed
            full = all_features(passed)
    kept = jnp.where(core == 0, blocks[0], blocks[1])
    received = shifted(jnp.where(core == 0, blocks[1], blocks[0]), "section")
    lower = jnp.where(core == 0, kept, received)
    upper = jnp.where(core == 0, received, kept)
    result = jnp.concatenate([lower, upper], 1).reshape(1, micro, row_count, features)
    steer_own = lax.psum(steer_part, "col")
    steer_other = shifted(steer_own, "section")
    steer_total = jnp.concatenate(
        [jnp.where(core == 0, steer_own, steer_other), jnp.where(core == 0, steer_other, steer_own)]
    )
    return (result, steer_total / (MICRO * ROWS))


CHUNKS = 4


def relay_kernel(
    u, w, hidden, gains, steer, lay, lay_row, res, steer_out, wg, q, xc, w1, partial, total, got, hv, gain_of, sums_of, stat, curve, coef,
    steer_acc, steer_all, own_sem, w1_sem, half_send, x1_send, x1_recv, a_send, a_recv, a_local, x2_send, x2_recv,
    c_send, c_recv, f_send, f_recv, w_send, w_recv, y_send, y_recv, g_send, g_recv,
    hid_send, hid_recv, hid_local, gain_sem, gain_send, stat_send, stat_recv, curve_send, curve_recv, u_sem, p_send,
    p_recv, tile_sem, out_sem, out_send, s_send, s_recv, s_local, t_sem, t_send
):
    core, row, col, group = (lax.axis_index(name) for name in ("section", "row", "col", "groups"))
    tokens, features = u.shape
    micro = 2
    row_count = tokens // micro
    half = features // 2
    part = half // 2
    quarter = tokens // 4
    cols = 4
    last = cols - 1
    f32 = jnp.float32
    chunk = part // CHUNKS
    my_half = pl.ds(pl.multiple_of(core * half, half), half)
    other_half = pl.ds(pl.multiple_of((1 - core) * half, half), half)
    my_block = row * 2 + core
    end = (col == 0) | (col == last)
    mid = jnp.logical_not(end)
    others = [
        jnp.where(col < 2, last, 0),
        jnp.where(col < 2, last - 1, 1),
        jnp.where(col < 2, 1 - col, 5 - col),
    ]
    near = others[2]

    def batch(m):
        return pl.ds(m * row_count, row_count)

    barrier = pltpu.get_barrier_semaphore()
    peers = [{"col": (col + step) % cols} for step in range(1, cols)]
    peers += [{"row": 1 - row}, {"groups": 1 - group}, {"section": 1 - core}, {"row": 1 - row, "section": 1 - core}]
    for peer in peers:
        pl.semaphore_signal(barrier, inc=1, device_id=peer, device_id_type=MESH)
    pl.semaphore_wait(barrier, len(peers))

    late = []

    class Send:
        def __init__(self, src, dst, send, recv, device, when=None, instead=None):
            def copy_from(ref):
                return pltpu.make_async_remote_copy(
                    src_ref=ref, dst_ref=dst, send_sem=send, recv_sem=recv, device_id=device, device_id_type=MESH
                )

            self.copy = copy_from(src)
            self.when = when
            self.waited = False
            late.append(self)
            if instead is None:
                self.guarded(self.copy.start)
            else:
                pl.when(when & instead[0])(lambda: copy_from(instead[1]).start())
                pl.when(when & jnp.logical_not(instead[0]))(lambda: self.copy.start())

        def guarded(self, action):
            if self.when is None:
                action()
            else:
                pl.when(self.when)(lambda: action())

        def wait_send(self):
            if not self.waited:
                self.waited = True
                self.guarded(self.copy.wait_send)

    def arrived(ref, sem, when=None):
        copy = pltpu.make_async_remote_copy(
            src_ref=ref, dst_ref=ref, send_sem=sem, recv_sem=sem, device_id={"section": 1 - core}, device_id_type=MESH
        )
        if when is None:
            copy.wait_recv()
        else:
            pl.when(when)(lambda: copy.wait_recv())

    for order in range(2):
        h = (group + order) % 2
        mine, there = pl.ds(h * part, part), pl.ds(half + h * part, part)

        @pl.when(core == 0)
        def _():
            pltpu.make_async_remote_copy(
                src_ref=w.at[there], dst_ref=wg.at[col, mine], send_sem=half_send.at[order], recv_sem=own_sem.at[order],
                device_id={"section": 1 - core}, device_id_type=MESH,
            ).start()

        @pl.when(core == 1)
        def _():
            pltpu.make_async_remote_copy(
                src_ref=w.at[mine], dst_ref=w1.at[mine], send_sem=half_send.at[order], recv_sem=w1_sem.at[order],
                device_id={"section": 1 - core}, device_id_type=MESH,
            ).start()
            pltpu.make_async_copy(w.at[there], w1.at[mine], w1_sem.at[order]).start()

    def wait_own(order):
        mine = pl.ds(((group + order) % 2) * part, part)
        arrived(wg.at[col, mine], own_sem.at[order], core == 1)

    def wait_w1(order):
        mine = pl.ds(((group + order) % 2) * part, part)
        pltpu.make_async_copy(w.at[mine], w1.at[mine], w1_sem.at[order]).wait()

    my_rows = pl.ds(pl.multiple_of(my_block * quarter, 64), quarter)

    def columns_of(index):
        return pl.ds(pl.multiple_of((index % 2) * half, half), half)

    first_block = jnp.where(col < 2, 1, 0)
    there_rows = pl.ds(pl.multiple_of(((1 - row) * 2 + core) * quarter, 64), quarter)

    def send_x1(order):
        at = columns_of(first_block + order)
        return Send(u.at[there_rows, at], q.at[:, at], x1_send.at[order], x1_recv.at[order], {"row": 1 - row})

    def wait_x1(order):
        arrived(q.at[:, columns_of(first_block + order)], x1_recv.at[order])

    column_sends = []

    def to_col(index, from_own):
        there = col if index == last else others[index]
        here = (there // 2) == row
        src = u.at[my_rows, columns_of(there)] if from_own else q.at[:, columns_of(there)]
        when = here if from_own else jnp.logical_not(here)
        dst = xc.at[col, my_rows]
        if index == last:
            pl.when(when)(lambda: pltpu.make_async_copy(src, dst, a_local).start())
        else:
            column_sends.append(
                Send(src, dst, a_send.at[index, int(from_own)], a_recv.at[col], {"col": there}, when)
            )

    def source_of(index):
        return col if index == last else others[index]

    def quarter_rows(row_at, core_at):
        return pl.ds(pl.multiple_of((row_at * 2 + core_at) * quarter, 64), quarter)

    token_sends = []

    def gather(index):
        ref = xc.at[source_of(index), my_rows]
        if index == last:
            pltpu.make_async_copy(ref, ref, a_local).wait()
        else:
            arrived(ref, a_recv.at[source_of(index)])
        token_sends.append(Send(ref, ref, x2_send.at[index], x2_recv.at[index], {"row": 1 - row}))
        token_sends.append(Send(ref, ref, c_send.at[index], c_recv.at[index], {"section": 1 - core}))

    def gather_rest(index):
        ref = xc.at[source_of(index), quarter_rows(1 - row, core)]
        arrived(ref, x2_recv.at[index])
        token_sends.append(Send(ref, ref, f_send.at[index], f_recv.at[index], {"section": 1 - core}))
        arrived(xc.at[source_of(index), quarter_rows(row, 1 - core)], c_recv.at[index])
        arrived(xc.at[source_of(index), quarter_rows(1 - row, 1 - core)], f_recv.at[index])

    queues = {"in": [], "mid": [], "out": [], "y_end": [], "y_mid": []}

    def queued(name, make):
        queue = queues[name]
        if len(queue) > 1:
            queue[-2].wait_send()
        queue.append(make())
        return queue[-1]

    def w_rows(k, of_group=None):
        return pl.ds(pl.multiple_of((group if of_group is None else of_group) * part + k * chunk, chunk), chunk)

    kinds = {
        "in": ("in", end, col, near, 0),
        "mid_own": ("mid", mid, col, last - col, 1),
        "out_own": ("out", mid, col, near, 0),
        "out_far": ("out", mid, others[1], near, 1),
        "mid_end": ("mid", mid, near, last - col, 2),
        "out_end": ("out", mid, others[0], near, 2),
    }
    places = list(kinds)

    def weights_to(kind, k):
        name, when, source, there, slot = kinds[kind]
        ref = wg.at[source, w_rows(k)]
        own = kind in ("in", "mid_own", "out_own")

        def make():
            return Send(
                ref, ref, w_send.at[places.index(kind), k], w_recv.at[slot, k], {"col": there}, when,
                (core == 0, w.at[w_rows(k)]) if own else None,
            )

        queued(name, make)

    def weights_in(slot, k, who):
        ref = wg.at[others[2 - slot], w_rows(k)]
        when = end if who == "end" else mid
        arrived(ref, w_recv.at[slot, k], when)
        queued(
            "y_" + who, lambda: Send(ref, ref, y_send.at[slot, k], y_recv.at[slot, k], {"groups": 1 - group}, when)
        )

    def y_arrived(slot, k):
        arrived(wg.at[others[2 - slot], w_rows(k, 1 - group)], y_recv.at[slot, k])

    tile = 256

    def multiply(index):
        @pl.loop(0, half // tile)
        def _(block):
            at = pl.ds(pl.multiple_of(block * tile, tile), tile)
            value = lax.dot_general(
                xc[source_of(index)], w1[at, :], (((1,), (1,)), ((), ())), preferred_element_type=f32
            )
            if index == last:
                total[:, at] = value
            else:
                partial[index, :, at] = value.astype(jnp.bfloat16)

    def add(dst, src, m, when):
        @pl.when(when)
        def _():
            @pl.loop(0, row_count // 32)
            def _(block):
                at = pl.ds(pl.multiple_of(m * row_count + block * 32, 32), 32)
                dst[at, :] = (dst[at, :].astype(f32) + src[at, :].astype(f32)).astype(dst.dtype)

    sum_sends = [[], []]

    def end_sum(index, m):
        send = queued(
            "in",
            lambda: Send(
                partial.at[index, batch(m)], got.at[index, batch(m)], g_send.at[index, m, 0], g_recv.at[index, m],
                {"col": near}, end,
            ),
        )
        sum_sends[m].append(send)

    def mid_sum(index, m):
        slot, to_slot = ((0, 3), (1, 4), (3, 2))[index]
        arrived(got.at[slot, batch(m)], g_recv.at[slot, m], mid)
        add(partial.at[index], got.at[slot], m, mid)
        send = queued(
            "out" if index == 2 else "mid",
            lambda: Send(
                partial.at[index, batch(m)], got.at[to_slot, batch(m)], g_send.at[index, m, 1], g_recv.at[to_slot, m],
                {"col": near if index == 2 else last - col}, mid,
            ),
        )
        sum_sends[m].append(send)

    def finish(m):
        arrived(got.at[4, batch(m)], g_recv.at[4, m], mid)
        add(total, got.at[4], m, mid)
        arrived(got.at[2, batch(m)], g_recv.at[2, m])
        add(total, got.at[2], m, col >= 0)

    def hidden_copies():
        for section in range(2):
            @pl.when(core == section)
            def _():
                for m in range(micro):
                    pltpu.make_async_copy(hidden.at[batch(m), my_half], hv.at[section, batch(m)], hid_local.at[m]).start()
                    pltpu.make_async_remote_copy(
                        src_ref=hidden.at[batch(m), other_half], dst_ref=hv.at[section, batch(m)], send_sem=hid_send.at[m],
                        recv_sem=hid_recv.at[m], device_id={"section": 1 - core}, device_id_type=MESH,
                    ).start()
                pltpu.make_async_copy(gains.at[:, my_half], gain_of.at[section], gain_sem.at[0]).start()
                pltpu.make_async_remote_copy(
                    src_ref=gains.at[:, other_half], dst_ref=gain_of.at[section], send_sem=gain_send,
                    recv_sem=gain_sem.at[1], device_id={"section": 1 - core}, device_id_type=MESH,
                ).start()

    def hidden_wait():
        for m in range(micro):
            pltpu.make_async_copy(hidden.at[batch(m), my_half], hv.at[0, batch(m)], hid_local.at[m]).wait()
            arrived(hv.at[0, batch(m)], hid_recv.at[m])
        pltpu.make_async_copy(gains.at[:, my_half], gain_of.at[0], gain_sem.at[0]).wait()
        arrived(gain_of.at[0], gain_sem.at[1])

    def hidden_sent():
        for m in range(micro):
            pltpu.make_async_remote_copy(
                src_ref=hidden.at[batch(m), other_half], dst_ref=hv.at[0, batch(m)], send_sem=hid_send.at[m],
                recv_sem=hid_recv.at[m], device_id={"section": 1 - core}, device_id_type=MESH,
            ).wait_send()
        pltpu.make_async_remote_copy(
            src_ref=gains.at[:, other_half], dst_ref=gain_of.at[0], send_sem=gain_send, recv_sem=gain_sem.at[1],
            device_id={"section": 1 - core}, device_id_type=MESH,
        ).wait_send()

    quad = [{"row": 1 - row}, {"section": 1 - core}, {"row": 1 - row, "section": 1 - core}]
    block_rows, block_cols = 16, 512
    lane = lax.broadcasted_iota(jnp.int32, (block_rows, 128), 1)

    def spread(values):
        result = jnp.zeros((block_rows, 128), f32)
        for index, value in enumerate(values):
            result = jnp.where(lane == index, value, result)
        return result

    def row_blocks(m, body):
        @pl.loop(0, row_count // block_rows)
        def _(index):
            body(pl.ds(pl.multiple_of(m * row_count + index * block_rows, block_rows), block_rows))

    def column_blocks():
        for index in range(half // block_cols):
            here = pl.ds(index * block_cols, block_cols)
            there = pl.ds(pl.multiple_of(core * half + index * block_cols, block_cols), block_cols)
            yield here, steer[0:1, there]

    def row_sum(value):
        return jnp.sum(value, -1, keepdims=True)

    def turned(m, there):
        for block in range(row_count // 128):
            at = slice(m * row_count + block * 128, m * row_count + (block + 1) * 128)
            there[0, :, at] = jnp.transpose(sums_of[at, :])[:8]

    def statistics(m):
        def body(at):
            sums = [jnp.zeros((block_rows, block_cols), f32) for _ in range(4)]
            for here, vector in column_blocks():
                for section in range(2):
                    plain = hv[section, at, here].astype(f32)
                    moved = plain + vector
                    sums[2 * section] += plain * plain
                    sums[2 * section + 1] += moved * moved
            sums_of[at, :] = spread([row_sum(value) for value in sums])

        row_blocks(m, body)
        turned(m, stat)
        for index, peer in enumerate(quad):
            Send(stat.at[0, :, batch(m)], stat.at[index + 1, :, batch(m)], stat_send.at[m, index], stat_recv.at[m, index], peer)

    def statistics_wait(m):
        for index in range(3):
            arrived(stat.at[index + 1, :, batch(m)], stat_recv.at[m, index])

    def load_upstream(m):
        pltpu.make_async_copy(u.at[batch(m), my_half], got.at[0, batch(m)], u_sem.at[m]).start()

    curve_sends = {}

    def curvature(section, m):
        incoming = got.at[0] if section == 1 else xc.at[my_block]
        for send in curve_sends.get(m, []):
            send.wait_send()

        def body(at):
            steered = lay[at, 0:1] == float(section)
            curved = jnp.zeros((block_rows, block_cols), f32)
            inner = jnp.zeros((block_rows, block_cols), f32)
            for here, vector in column_blocks():
                plain = hv[section, at, here].astype(f32)
                moved = plain + vector
                scaled = gain_of[section, 0:1, here] * total[at, here]
                curved += scaled * jnp.where(steered, moved, plain)
                inner += incoming[at, here].astype(f32) * moved
            sums_of[at, :] = spread([row_sum(curved), row_sum(inner)])

        row_blocks(m, body)
        turned(m, curve)
        curve_sends[m] = [
            Send(
                curve.at[0, :, batch(m)], curve.at[index + 1, :, batch(m)], curve_send.at[section, m, index],
                curve_recv.at[section, m, index], peer,
            )
            for index, peer in enumerate(quad)
        ]

    def gradient(section, m, out):
        for index in range(3):
            arrived(curve.at[index + 1, :, batch(m)], curve_recv.at[section, m, index])
        if section == 1:
            statistics_wait(m)
        span = 128
        for block in range(row_count // span):
            at = slice(m * row_count + block * span, m * row_count + (block + 1) * span)
            both = (curve[0, :, at] + curve[1, :, at]) + (curve[2, :, at] + curve[3, :, at])
            sums = (stat[0, :, at] + stat[1, :, at]) + (stat[2, :, at] + stat[3, :, at])
            curved, inner = both[0:1], both[1:2]
            plain_sq, moved_sq = sums[2 * section : 2 * section + 1], sums[2 * section + 1 : 2 * section + 2]
            steered = lay_row[0:1, at] == float(section)
            norm_plain = jnp.sqrt(plain_sq + epsilon)
            norm_moved = jnp.sqrt(moved_sq + epsilon)
            rescale = norm_plain / norm_moved
            square_sum = jnp.where(
                steered, norm_plain * norm_plain * moved_sq / (norm_moved * norm_moved), plain_sq
            )
            root_mean = jnp.sqrt(square_sum / D + epsilon)
            scale = jnp.where(steered, rescale, 1.0)
            factor = scale * curved / (D * (root_mean * root_mean * root_mean))
            radial = (inner + curved / root_mean - rescale * factor * moved_sq) / norm_moved
            wide = lax.broadcasted_iota(jnp.int32, (span, span), 0)
            result = jnp.zeros((span, span), f32)
            terms = (1.0 / root_mean, scale * factor, rescale, radial / norm_moved, radial / norm_plain)
            for place, value in enumerate(terms):
                result = jnp.where(wide == place, value, result)
            coef[at, :] = jnp.transpose(result)

        incoming = got.at[0] if section == 1 else xc.at[my_block]

        def body(at):
            steered = lay[at, 0:1] == float(section)
            inverse, pull, rescale, along, back = [coef[at, place : place + 1] for place in range(5)]
            for here, vector in column_blocks():
                plain = hv[section, at, here].astype(f32)
                moved = plain + vector
                scaled = gain_of[section, 0:1, here] * total[at, here]
                grad = incoming[at, here].astype(f32) + scaled * inverse - jnp.where(steered, moved, plain) * pull
                tangent = rescale * (grad - moved * along)
                out[at, here] = jnp.where(steered, tangent + plain * back, grad).astype(jnp.bfloat16)
                kept = jnp.where(steered, tangent, 0.0)
                steer_acc[:, here] += kept[:8] + kept[8:]

        row_blocks(m, body)
        @pl.when(core == section)
        def _():
            pltpu.make_async_copy(out.at[batch(m)], res.at[batch(m), my_half], out_sem.at[0, m]).start()

        @pl.when(core != section)
        def _():
            pltpu.make_async_remote_copy(
                src_ref=out.at[batch(m)], dst_ref=res.at[batch(m), my_half], send_sem=out_send.at[m], recv_sem=out_sem.at[1, m],
                device_id={"section": 1 - core}, device_id_type=MESH,
            ).start()

    def out_wait(section, m):
        pltpu.make_async_remote_copy(
            src_ref=partial.at[0, batch(m)], dst_ref=res.at[batch(m), my_half], send_sem=out_send.at[m], recv_sem=out_sem.at[1, m],
            device_id={"section": 1 - core}, device_id_type=MESH,
        ).wait_send()

    def pass_down(m):
        ref = xc.at[my_block, batch(m)]
        Send(ref, ref, p_send.at[m, 0], p_recv.at[m, 0], {"row": 1 - row})
        Send(ref, ref, p_send.at[m, 1], p_recv.at[m, 1], {"section": 1 - core})

    def pass_on(m):
        ref = xc.at[(1 - row) * 2 + core, batch(m)]
        arrived(ref, p_recv.at[m, 0])
        Send(ref, ref, p_send.at[m, 2], p_recv.at[m, 2], {"section": 1 - core})

    def pass_wait(m):
        arrived(xc.at[row * 2 + 1 - core, batch(m)], p_recv.at[m, 1])
        arrived(xc.at[(1 - row) * 2 + 1 - core, batch(m)], p_recv.at[m, 2])

    def section_one(m):
        finish(m)
        for send in token_sends:
            send.wait_send()
        pltpu.make_async_copy(u.at[batch(m), my_half], got.at[0, batch(m)], u_sem.at[m]).wait()
        curvature(1, m)
        gradient(1, m, xc.at[my_block])
        pass_down(m)

    width = chunk
    own_tiles = half // width

    def early_tile(index):
        rest = jnp.maximum(index - own_tiles, 0)
        source = (col + 1 + rest // 4) % cols
        inside = rest % 4
        start = (inside // 2) * part + (inside % 2) * width
        own = index < own_tiles
        return jnp.where(own, col, source), jnp.where(own, index * width, start)

    def late_tile(k):
        def tile_of(index):
            return (col + 1 + index // 2) % cols, (index % 2) * part + k * width

        return tile_of

    def products(batches, count, tile_of, first):
        def load(index, own=False):
            source, start = tile_of(index)
            slot = index % 2
            rows = pl.ds(pl.multiple_of(start, width), width)
            return pltpu.make_async_copy(
                w.at[rows] if own else wg.at[source, rows],
                w1.at[pl.ds(pl.multiple_of(slot * width, width), width)],
                tile_sem.at[slot],
            )

        def load_start(index, when):
            own = (core == 0) & (index < own_tiles) if first else None
            if own is None:
                pl.when(when)(lambda: load(index).start())
            else:
                pl.when(when & own)(lambda: load(index, True).start())
                pl.when(when & jnp.logical_not(own))(lambda: load(index).start())

        load_start(jnp.int32(0), core >= 0)

        @pl.loop(0, count)
        def _(index):
            load_start(index + 1, index + 1 < count)
            load(index).wait()
            source, start = tile_of(index)
            rows = pl.ds(pl.multiple_of((index % 2) * width, width), width)
            at = pl.ds(pl.multiple_of(start, width), width)
            for m in batches:
                value = lax.dot_general(
                    xc[source, batch(m), :], w1[rows, :], (((1,), (1,)), ((), ())), preferred_element_type=f32
                )
                if first:
                    @pl.when(index < own_tiles)
                    def _():
                        total[batch(m), at] = value

                    @pl.when(index >= own_tiles)
                    def _():
                        total[batch(m), at] += value
                else:
                    total[batch(m), at] += value

    early_count = own_tiles + 12
    steer_acc[...] = jnp.zeros_like(steer_acc)

    first = send_x1(0)
    to_col(0, True)
    wait_own(0)
    for kind in ("in", "mid_own", "out_own"):
        weights_to(kind, 0)
    first.wait_send()
    send_x1(1)
    wait_x1(0)
    to_col(0, False)
    hidden_copies()
    wait_x1(1)
    for send in column_sends:
        send.wait_send()
    for index in (1, 2, last):
        to_col(index, True)
        to_col(index, False)
    gather(0)
    weights_to("in", 1)
    weights_to("mid_own", 1)
    weights_to("out_own", 1)
    hidden_wait()
    statistics(0)
    gather(1)
    gather_rest(0)
    wait_w1(0)
    wait_w1(1)
    multiply(0)
    end_sum(0, 0)
    weights_in(0, 0, "end")
    weights_in(1, 0, "mid")
    end_sum(0, 1)
    gather(2)
    gather(last)
    gather_rest(1)
    multiply(1)
    weights_to("out_own", 2)
    gather_rest(2)
    multiply(2)
    gather_rest(last)
    multiply(last)
    end_sum(1, 0)
    mid_sum(0, 0)
    load_upstream(0)
    weights_in(0, 0, "mid")
    weights_in(0, 1, "end")
    statistics(1)
    weights_to("out_own", 3)
    end_sum(1, 1)
    mid_sum(0, 1)
    load_upstream(1)
    weights_in(1, 1, "mid")
    weights_to("mid_own", 2)
    weights_to("out_far", 0)
    mid_sum(2, 0)
    weights_to("in", 2)
    mid_sum(1, 0)
    weights_in(0, 1, "mid")
    weights_in(0, 2, "end")
    weights_to("out_far", 1)
    end_sum(2, 0)
    weights_to("mid_end", 0)
    mid_sum(2, 1)
    mid_sum(1, 1)
    weights_in(1, 2, "mid")
    weights_in(0, 3, "end")
    weights_to("out_far", 2)
    end_sum(2, 1)
    weights_to("mid_own", 3)
    weights_in(0, 2, "mid")
    weights_in(1, 0, "end")
    weights_in(2, 0, "mid")
    weights_to("out_end", 0)
    weights_to("in", 3)
    weights_to("mid_end", 1)
    section_one(0)
    weights_in(1, 1, "end")
    weights_in(1, 3, "mid")
    weights_to("out_far", 3)
    weights_to("mid_end", 2)
    section_one(1)
    pass_on(0)
    weights_in(1, 2, "end")
    weights_in(2, 1, "mid")
    weights_to("out_end", 1)
    weights_in(0, 3, "mid")
    weights_to("mid_end", 3)
    weights_in(2, 0, "end")
    pass_on(1)
    weights_in(2, 2, "mid")
    weights_to("out_end", 2)
    weights_in(1, 3, "end")
    wait_own(1)
    pass_wait(0)
    weights_in(2, 1, "end")
    for k in range(2):
        for slot in range(3):
            y_arrived(slot, k)
    products([0], early_count, early_tile, True)
    weights_in(2, 3, "mid")
    weights_to("out_end", 3)
    weights_in(2, 2, "end")
    pass_wait(1)
    products([1], early_count, early_tile, True)
    for slot in range(3):
        y_arrived(slot, 2)
    products([0, 1], 6, late_tile(2), False)
    weights_in(2, 3, "end")
    for slot in range(3):
        y_arrived(slot, 3)
    products([0, 1], 6, late_tile(3), False)
    for m in range(micro):
        for send in sum_sends[m]:
            send.wait_send()
    for m in range(micro):
        pl.when(core == 0)(lambda: out_wait(1, m))
        curvature(0, m)
    for m in range(micro):
        gradient(0, m, partial.at[0])

    own_copy = pltpu.make_async_copy(steer_acc, steer_all.at[col], s_local)
    own_copy.start()
    for step in range(1, cols):
        there = (col + step) % cols
        Send(steer_acc, steer_all.at[col], s_send.at[step], s_recv.at[step], {"col": there})
    own_copy.wait()
    for step in range(1, cols):
        arrived(steer_all.at[(col - step) % cols], s_recv.at[step])
    for send in late:
        send.wait_send()
    steer_acc[...] = (steer_all[0] + steer_all[1]) + (steer_all[2] + steer_all[3])
    final = pltpu.make_async_copy(steer_acc, steer_out.at[core], t_sem.at[0])
    final.start()
    give = pltpu.make_async_remote_copy(
        src_ref=steer_acc, dst_ref=steer_out.at[core], send_sem=t_send, recv_sem=t_sem.at[1],
        device_id={"section": 1 - core}, device_id_type=MESH,
    )
    give.start()
    final.wait()
    give.wait()

    for order in range(2):
        pltpu.make_async_remote_copy(
            src_ref=w.at[pl.ds(0, part)], dst_ref=wg.at[col, pl.ds(0, part)], send_sem=half_send.at[order],
            recv_sem=own_sem.at[order], device_id={"section": 1 - core}, device_id_type=MESH,
        ).wait_send()
    hidden_sent()
    for m in range(micro):
        pltpu.make_async_copy(partial.at[0, batch(m)], res.at[batch(m), my_half], out_sem.at[0, m]).wait()
        arrived(res.at[batch(m), other_half], out_sem.at[1, m])
        pl.when(core == 1)(lambda: out_wait(0, m))


def relay(u, w, hidden, gains, steer, lay, lay_row):
    tokens, features = u.shape
    micro = 2
    half = features // 2
    dma = pltpu.SemaphoreType.DMA
    bf16, f32 = jnp.bfloat16, jnp.float32
    in_vmem = pl.BlockSpec(memory_space=pltpu.VMEM)
    anywhere = pl.BlockSpec(memory_space=pl.ANY)
    return pl.pallas_call(
        relay_kernel,
        out_shape=(
            jax.ShapeDtypeStruct((tokens, features), bf16),
            jax.ShapeDtypeStruct((2, 8, half), f32),
            jax.ShapeDtypeStruct((4, half, half), bf16),
            jax.ShapeDtypeStruct((tokens // 4, features), bf16),
        ),
        in_specs=[anywhere, anywhere, anywhere, anywhere, in_vmem, in_vmem, in_vmem],
        out_specs=(anywhere,) * 4,
        scratch_shapes=[
            pltpu.VMEM((4, tokens, half), bf16),
            pltpu.VMEM((half, half), bf16),
            pltpu.VMEM((3, tokens, half), bf16),
            pltpu.VMEM((tokens, half), f32),
            pltpu.VMEM((5, tokens, half), bf16),
            pltpu.VMEM((2, tokens, half), bf16),
            pltpu.VMEM((2, 8, half), f32),
            pltpu.VMEM((tokens, 128), f32),
            pltpu.VMEM((4, 8, tokens), f32),
            pltpu.VMEM((4, 8, tokens), f32),
            pltpu.VMEM((tokens, 128), f32),
            pltpu.VMEM((8, half), f32),
            pltpu.VMEM((4, 8, half), f32),
            dma((2,)), dma((2,)), dma((2,)),
            dma((2,)), dma((2,)),
            dma((3, 2)), dma((4,)), dma,
            dma((4,)), dma((4,)), dma((4,)), dma((4,)), dma((4,)), dma((4,)),
            dma((6, CHUNKS)), dma((3, CHUNKS)), dma((3, CHUNKS)), dma((3, CHUNKS)),
            dma((3, 2, 2)), dma((5, 2)),
            dma((2,)), dma((2,)), dma((2,)), dma((2,)), dma,
            dma((2, 3)), dma((2, 3)),
            dma((2, 2, 3)), dma((2, 2, 3)),
            dma((2,)),
            dma((2, 3)), dma((2, 3)),
            dma((2,)),
            dma((2, 2)), dma((2,)),
            dma((4,)), dma((4,)), dma, dma((2,)), dma,
        ],
        compiler_params=pltpu.CompilerParams(
            collective_id=0, has_side_effects=True, vmem_limit_bytes=63 * 1024 * 1024
        ),
        cost_estimate=pl.CostEstimate(
            flops=4 * 4 * tokens * half * half, bytes_accessed=150 * 1024 * 1024, transcendentals=0
        ),
        name="relay",
    )(u, w, hidden, gains, steer, lay, lay_row)


def shared_weights(hidden, upstream, weights, norm_gains, steering, steer_layer):
    micro, row_count, features = upstream.shape
    tokens = micro * row_count
    f32 = jnp.float32
    gains = jnp.broadcast_to(norm_gains[0].astype(f32), (8, features))
    steer = jnp.broadcast_to(steering.astype(f32), (8, features))
    lay = jnp.broadcast_to(steer_layer.reshape(tokens).astype(f32)[:, None], (tokens, 128))
    lay_row = jnp.broadcast_to(steer_layer.reshape(tokens).astype(f32), (8, tokens))
    result, steer_parts, _, _ = relay(
        upstream.reshape(tokens, features), weights[0], hidden[0].reshape(tokens, features), gains, steer, lay, lay_row
    )
    steer_total = jnp.sum(steer_parts, 1).reshape(features)
    return (result.reshape(1, micro, row_count, features), steer_total / (MICRO * ROWS))


def solution(mesh):
    placed = (
        P("section", None, ("groups", "col"), "row"),
        P(None, ("groups", "col"), "row"),
        P("section", "row", "col"),
        P("section", "row"),
        P(("groups", "row")),
        P(None, ("groups", "col")),
    )
    small = mesh.shape["row"] == 2 and mesh.shape["col"] == 4 and mesh.shape["groups"] == 2
    return jax.shard_map(
        shared_weights if small else local,
        mesh=mesh,
        in_specs=placed,
        out_specs=(P("section", None, ("groups", "col"), "row"), P(("groups", "row"))),
        check_vma=False,
    )
```

```python
import jax
import jax.numpy as jnp
from jax import lax
from jax.experimental import pallas as pl
from jax.experimental.pallas import tpu as pltpu
from jax.sharding import PartitionSpec as P

D = 8192
ROWS = 1536
MICRO = 2


epsilon = 1e-06
MESH = pl.DeviceIdType.MESH


def shifted(value, axis, steps=1):
    count = lax.axis_size(axis)
    return lax.ppermute(value, axis, [(source, (source + steps) % count) for source in range(count)])


def columns(value, start, width):
    return lax.dynamic_slice_in_dim(value, start, width, value.ndim - 1)


def after(value, earlier):
    return lax.optimization_barrier((value, earlier))[0]


def local(hidden, upstream, weights, norm_gains, steering, steer_layer):
    core = lax.axis_index("section")
    row_index = lax.axis_index("row")
    col_index = lax.axis_index("col")
    group = lax.axis_index("groups")
    row_devices = lax.axis_size("row")
    cols = lax.axis_size("col")
    groups = lax.axis_size("groups")
    micro, row_count, features = upstream.shape
    tokens = micro * row_count
    half = features // 2
    depth = weights.shape[2]
    part = depth // groups
    f32 = jnp.float32

    def own_columns(value):
        return columns(value, core * half, half)

    def per_section(mine, received):
        return jnp.where(core == 0, mine, received), jnp.where(core == 1, mine, received)

    def over_cores(value, axis):
        mine = lax.dynamic_slice_in_dim(value, core * half, half, axis)
        given = lax.dynamic_slice_in_dim(value, (1 - core) * half, half, axis)
        return per_section(mine, shifted(given, "section"))

    units = max(1, part // 128)
    step_units = max(1, units // 4)
    unit = part // units
    widths_of = {}
    for section in (1, 0):
        sizes = [step_units] * (units // step_units)
        if sum(sizes) < units:
            sizes.append(units - sum(sizes))
        widths_of[section] = [size * unit for size in sizes]
    mine = lax.dynamic_slice_in_dim(weights[0], core * half, half, 0)
    given = lax.dynamic_slice_in_dim(weights[0], (1 - core) * half, half, 0)
    lead = sum(widths_of[1][:2])
    lead_given = shifted(columns(given, group * part, lead), "section")
    first_pieces = per_section(columns(mine, group * part, lead), lead_given)
    weight_of = per_section(mine, shifted(after(given, lead_given), "section"))
    hidden_of = over_cores(hidden[0].reshape(tokens, features), 1)
    gain_of = over_cores(norm_gains[0], 0)
    steer_vec = own_columns(steering).astype(f32)
    layers = steer_layer.reshape(tokens)
    upstream_rows = upstream.reshape(tokens, features)

    earlier, sent = [], []
    pieces = {}
    for section in (1, 0):
        held = []
        start = 0
        for width in widths_of[section]:
            if start + width <= lead:
                own = first_pieces[section][:, start : start + width]
            else:
                own = columns(weight_of[section], group * part + start, width)
            if earlier:
                own = after(own, tuple(earlier))
            gathered = lax.all_gather(own, "col", axis=1, tiled=True)
            others = jnp.concatenate(
                [columns(gathered, ((col_index + step) % cols) * width, width) for step in range(1, cols)], 1
            )
            held.append((start, width, (others, shifted(others, "groups"))))
            earlier = [others] + sent[-1:]
            sent.append(held[-1][2][1])
            start += width
        pieces[section] = held

    def projected(full, section):
        def times(left, right):
            return lax.dot_general(left, right, (((1,), (1,)), ((), ())), preferred_element_type=f32)

        total = times(columns(full, col_index * depth, depth), weight_of[section])
        held = pieces[section]
        for start, width, sides in held:
            total = lax.optimization_barrier(total)
            for side, block in enumerate(sides):
                offset = ((group + side) % groups) * part + start
                left = jnp.concatenate(
                    [columns(full, ((col_index + step) % cols) * depth + offset, width) for step in range(1, cols)], 1
                )
                total = total + times(left, block)
        return total

    def all_features(own):
        if row_devices == 2:
            other = shifted(own, "row")
            both = jnp.concatenate([jnp.where(row_index == 0, own, other), jnp.where(row_index == 0, other, own)], 1)
            if own.shape[1] == features:
                return both
            there = shifted(both, "section")
            lower = jnp.where(core == 0, both, there)
            upper = jnp.where(core == 0, there, both)
            return jnp.concatenate([lower[:, :half], upper[:, :half], lower[:, half:], upper[:, half:]], 1)
        if own.shape[1] == features:
            return lax.all_gather(own, "row", axis=1, tiled=True)
        return lax.all_gather(own, ("row", "section"), axis=1, tiled=True)

    local_sums = []
    for section in range(2):
        unsteered = hidden_of[section].astype(f32)
        moved = unsteered + steer_vec
        local_sums += [jnp.sum(unsteered * unsteered, -1), jnp.sum(moved * moved, -1)]
    sums = lax.psum(tuple(local_sums), ("row", "section"))

    incoming = own_columns(upstream_rows)
    full = all_features(upstream_rows)
    steer_part = jnp.zeros((half,), f32)
    blocks = [None, None]
    for section in (1, 0):
        plain_sq, moved_sq = sums[2 * section], sums[2 * section + 1]
        steered = layers == section
        steered_col = steered[:, None]
        unsteered = hidden_of[section].astype(f32)
        moved = unsteered + steer_vec
        grad_float = incoming.astype(f32)
        scaled = gain_of[section].astype(f32) * projected(full, section)
        chosen = jnp.where(steered_col, moved, unsteered)
        curve, inner = lax.psum(
            (jnp.sum(scaled * chosen, -1), jnp.sum(grad_float * moved, -1)), ("row", "section")
        )
        norm_plain = jnp.sqrt(plain_sq + epsilon)
        norm_moved = jnp.sqrt(moved_sq + epsilon)
        rescale = norm_plain / norm_moved
        square_sum = jnp.where(
            steered, norm_plain * norm_plain * moved_sq / (norm_moved * norm_moved), plain_sq
        )
        root_mean = jnp.sqrt(square_sum / D + epsilon)
        scale = jnp.where(steered, rescale, 1.0)
        factor = scale * curve / (D * root_mean**3)
        input_grad = grad_float + scaled / root_mean[:, None] - chosen * (scale * factor)[:, None]
        radial = (inner + curve / root_mean - rescale * factor * moved_sq) / norm_moved
        tangent = rescale[:, None] * (input_grad - moved * (radial / norm_moved)[:, None])
        below = jnp.where(steered_col, tangent + unsteered * (radial / norm_plain)[:, None], input_grad)
        passed = below.astype(jnp.bfloat16)
        blocks[section] = passed
        steer_part = steer_part + jnp.sum(jnp.where(steered_col, tangent, 0.0), 0)
        if section == 1:
            incoming = passed
            full = all_features(passed)
    kept = jnp.where(core == 0, blocks[0], blocks[1])
    received = shifted(jnp.where(core == 0, blocks[1], blocks[0]), "section")
    lower = jnp.where(core == 0, kept, received)
    upper = jnp.where(core == 0, received, kept)
    result = jnp.concatenate([lower, upper], 1).reshape(1, micro, row_count, features)
    steer_own = lax.psum(steer_part, "col")
    steer_other = shifted(steer_own, "section")
    steer_total = jnp.concatenate(
        [jnp.where(core == 0, steer_own, steer_other), jnp.where(core == 0, steer_other, steer_own)]
    )
    return (result, steer_total / (MICRO * ROWS))


CHUNKS = 4


def relay_kernel(
    u, w, hidden, gains, steer, lay, lay_row, res, steer_out, wg, q, xc, w1, partial, total, got, hv, gain_of, sums_of, stat, curve, coef,
    steer_acc, steer_all, own_sem, w1_sem, half_send, x1_send, x1_recv, a_send, a_recv, a_local, x2_send, x2_recv,
    c_send, c_recv, f_send, f_recv, w_send, w_recv, y_send, y_recv, g_send, g_recv,
    hid_send, hid_recv, hid_local, gain_sem, gain_send, stat_send, stat_recv, curve_send, curve_recv, u_sem, p_send,
    p_recv, tile_sem, out_sem, out_send, s_send, s_recv, s_local, t_sem, t_send
):
    core, row, col, group = (lax.axis_index(name) for name in ("section", "row", "col", "groups"))
    tokens, features = u.shape
    micro = 2
    row_count = tokens // micro
    half = features // 2
    part = half // 2
    quarter = tokens // 4
    cols = 4
    last = cols - 1
    f32 = jnp.float32
    chunk = part // CHUNKS
    my_half = pl.ds(pl.multiple_of(core * half, half), half)
    other_half = pl.ds(pl.multiple_of((1 - core) * half, half), half)
    my_block = row * 2 + core
    end = (col == 0) | (col == last)
    mid = jnp.logical_not(end)
    others = [
        jnp.where(col < 2, last, 0),
        jnp.where(col < 2, last - 1, 1),
        jnp.where(col < 2, 1 - col, 5 - col),
    ]
    near = others[2]

    def batch(m):
        return pl.ds(m * row_count, row_count)

    barrier = pltpu.get_barrier_semaphore()
    peers = [{"col": (col + step) % cols} for step in range(1, cols)]
    peers += [{"row": 1 - row}, {"groups": 1 - group}, {"section": 1 - core}, {"row": 1 - row, "section": 1 - core}]
    for peer in peers:
        pl.semaphore_signal(barrier, inc=1, device_id=peer, device_id_type=MESH)
    pl.semaphore_wait(barrier, len(peers))

    late = []

    class Send:
        def __init__(self, src, dst, send, recv, device, when=None, instead=None):
            def copy_from(ref):
                return pltpu.make_async_remote_copy(
                    src_ref=ref, dst_ref=dst, send_sem=send, recv_sem=recv, device_id=device, device_id_type=MESH
                )

            self.copy = copy_from(src)
            self.when = when
            self.waited = False
            late.append(self)
            if instead is None:
                self.guarded(self.copy.start)
            else:
                pl.when(when & instead[0])(lambda: copy_from(instead[1]).start())
                pl.when(when & jnp.logical_not(instead[0]))(lambda: self.copy.start())

        def guarded(self, action):
            if self.when is None:
                action()
            else:
                pl.when(self.when)(lambda: action())

        def wait_send(self):
            if not self.waited:
                self.waited = True
                self.guarded(self.copy.wait_send)

    def arrived(ref, sem, when=None):
        copy = pltpu.make_async_remote_copy(
            src_ref=ref, dst_ref=ref, send_sem=sem, recv_sem=sem, device_id={"section": 1 - core}, device_id_type=MESH
        )
        if when is None:
            copy.wait_recv()
        else:
            pl.when(when)(lambda: copy.wait_recv())

    for order in range(2):
        h = (group + order) % 2
        mine, there = pl.ds(h * part, part), pl.ds(half + h * part, part)

        @pl.when(core == 0)
        def _():
            pltpu.make_async_remote_copy(
                src_ref=w.at[there], dst_ref=wg.at[col, mine], send_sem=half_send.at[order], recv_sem=own_sem.at[order],
                device_id={"section": 1 - core}, device_id_type=MESH,
            ).start()

        @pl.when(core == 1)
        def _():
            pltpu.make_async_remote_copy(
                src_ref=w.at[mine], dst_ref=w1.at[mine], send_sem=half_send.at[order], recv_sem=w1_sem.at[order],
                device_id={"section": 1 - core}, device_id_type=MESH,
            ).start()
            pltpu.make_async_copy(w.at[there], w1.at[mine], w1_sem.at[order]).start()

    def wait_own(order):
        mine = pl.ds(((group + order) % 2) * part, part)
        arrived(wg.at[col, mine], own_sem.at[order], core == 1)

    def wait_w1(order):
        mine = pl.ds(((group + order) % 2) * part, part)
        pltpu.make_async_copy(w.at[mine], w1.at[mine], w1_sem.at[order]).wait()

    my_rows = pl.ds(pl.multiple_of(my_block * quarter, 64), quarter)

    def columns_of(index):
        return pl.ds(pl.multiple_of((index % 2) * half, half), half)

    first_block = jnp.where(col < 2, 1, 0)
    there_rows = pl.ds(pl.multiple_of(((1 - row) * 2 + core) * quarter, 64), quarter)

    def send_x1(order):
        at = columns_of(first_block + order)
        return Send(u.at[there_rows, at], q.at[:, at], x1_send.at[order], x1_recv.at[order], {"row": 1 - row})

    def wait_x1(order):
        arrived(q.at[:, columns_of(first_block + order)], x1_recv.at[order])

    column_sends = []

    def to_col(index, from_own):
        there = col if index == last else others[index]
        here = (there // 2) == row
        src = u.at[my_rows, columns_of(there)] if from_own else q.at[:, columns_of(there)]
        when = here if from_own else jnp.logical_not(here)
        dst = xc.at[col, my_rows]
        if index == last:
            pl.when(when)(lambda: pltpu.make_async_copy(src, dst, a_local).start())
        else:
            column_sends.append(
                Send(src, dst, a_send.at[index, int(from_own)], a_recv.at[col], {"col": there}, when)
            )

    def source_of(index):
        return col if index == last else others[index]

    def quarter_rows(row_at, core_at):
        return pl.ds(pl.multiple_of((row_at * 2 + core_at) * quarter, 64), quarter)

    token_sends = []

    def gather(index):
        ref = xc.at[source_of(index), my_rows]
        if index == last:
            pltpu.make_async_copy(ref, ref, a_local).wait()
        else:
            arrived(ref, a_recv.at[source_of(index)])
        token_sends.append(Send(ref, ref, x2_send.at[index], x2_recv.at[index], {"row": 1 - row}))
        token_sends.append(Send(ref, ref, c_send.at[index], c_recv.at[index], {"section": 1 - core}))

    def gather_rest(index):
        ref = xc.at[source_of(index), quarter_rows(1 - row, core)]
        arrived(ref, x2_recv.at[index])
        token_sends.append(Send(ref, ref, f_send.at[index], f_recv.at[index], {"section": 1 - core}))
        arrived(xc.at[source_of(index), quarter_rows(row, 1 - core)], c_recv.at[index])
        arrived(xc.at[source_of(index), quarter_rows(1 - row, 1 - core)], f_recv.at[index])

    queues = {"in": [], "mid": [], "out": [], "y_end": [], "y_mid": []}

    def queued(name, make):
        queue = queues[name]
        if len(queue) > 2:
            queue[-3].wait_send()
        queue.append(make())
        return queue[-1]

    def w_rows(k, of_group=None):
        return pl.ds(pl.multiple_of((group if of_group is None else of_group) * part + k * chunk, chunk), chunk)

    kinds = {
        "in": ("in", end, col, near, 0),
        "mid_own": ("mid", mid, col, last - col, 1),
        "out_own": ("out", mid, col, near, 0),
        "out_far": ("out", mid, others[1], near, 1),
        "mid_end": ("mid", mid, near, last - col, 2),
        "out_end": ("out", mid, others[0], near, 2),
    }
    places = list(kinds)

    def weights_to(kind, k):
        name, when, source, there, slot = kinds[kind]
        ref = wg.at[source, w_rows(k)]
        own = kind in ("in", "mid_own", "out_own")

        def make():
            return Send(
                ref, ref, w_send.at[places.index(kind), k], w_recv.at[slot, k], {"col": there}, when,
                (core == 0, w.at[w_rows(k)]) if own else None,
            )

        queued(name, make)

    def weights_in(slot, k, who):
        ref = wg.at[others[2 - slot], w_rows(k)]
        when = end if who == "end" else mid
        arrived(ref, w_recv.at[slot, k], when)
        queued(
            "y_" + who, lambda: Send(ref, ref, y_send.at[slot, k], y_recv.at[slot, k], {"groups": 1 - group}, when)
        )

    def y_arrived(slot, k):
        arrived(wg.at[others[2 - slot], w_rows(k, 1 - group)], y_recv.at[slot, k])

    tile = 256

    def multiply(index):
        @pl.loop(0, half // tile)
        def _(block):
            at = pl.ds(pl.multiple_of(block * tile, tile), tile)
            value = lax.dot_general(
                xc[source_of(index)], w1[at, :], (((1,), (1,)), ((), ())), preferred_element_type=f32
            )
            if index == last:
                total[:, at] = value
            else:
                partial[index, :, at] = value.astype(jnp.bfloat16)

    def add(dst, src, m, when):
        @pl.when(when)
        def _():
            @pl.loop(0, row_count // 32)
            def _(block):
                at = pl.ds(pl.multiple_of(m * row_count + block * 32, 32), 32)
                dst[at, :] = (dst[at, :].astype(f32) + src[at, :].astype(f32)).astype(dst.dtype)

    sum_sends = [[], []]

    def end_sum(index, m):
        send = queued(
            "in",
            lambda: Send(
                partial.at[index, batch(m)], got.at[index, batch(m)], g_send.at[index, m, 0], g_recv.at[index, m],
                {"col": near}, end,
            ),
        )
        sum_sends[m].append(send)

    def mid_sum(index, m):
        slot, to_slot = ((0, 3), (1, 4), (3, 2))[index]
        arrived(got.at[slot, batch(m)], g_recv.at[slot, m], mid)
        add(partial.at[index], got.at[slot], m, mid)
        send = queued(
            "out" if index == 2 else "mid",
            lambda: Send(
                partial.at[index, batch(m)], got.at[to_slot, batch(m)], g_send.at[index, m, 1], g_recv.at[to_slot, m],
                {"col": near if index == 2 else last - col}, mid,
            ),
        )
        sum_sends[m].append(send)

    def finish(m):
        arrived(got.at[4, batch(m)], g_recv.at[4, m], mid)
        add(total, got.at[4], m, mid)
        arrived(got.at[2, batch(m)], g_recv.at[2, m])
        add(total, got.at[2], m, col >= 0)

    def hidden_copies():
        for section in range(2):
            @pl.when(core == section)
            def _():
                for m in range(micro):
                    pltpu.make_async_copy(hidden.at[batch(m), my_half], hv.at[section, batch(m)], hid_local.at[m]).start()
                    pltpu.make_async_remote_copy(
                        src_ref=hidden.at[batch(m), other_half], dst_ref=hv.at[section, batch(m)], send_sem=hid_send.at[m],
                        recv_sem=hid_recv.at[m], device_id={"section": 1 - core}, device_id_type=MESH,
                    ).start()
                pltpu.make_async_copy(gains.at[:, my_half], gain_of.at[section], gain_sem.at[0]).start()
                pltpu.make_async_remote_copy(
                    src_ref=gains.at[:, other_half], dst_ref=gain_of.at[section], send_sem=gain_send,
                    recv_sem=gain_sem.at[1], device_id={"section": 1 - core}, device_id_type=MESH,
                ).start()

    def hidden_wait():
        for m in range(micro):
            pltpu.make_async_copy(hidden.at[batch(m), my_half], hv.at[0, batch(m)], hid_local.at[m]).wait()
            arrived(hv.at[0, batch(m)], hid_recv.at[m])
        pltpu.make_async_copy(gains.at[:, my_half], gain_of.at[0], gain_sem.at[0]).wait()
        arrived(gain_of.at[0], gain_sem.at[1])

    def hidden_sent():
        for m in range(micro):
            pltpu.make_async_remote_copy(
                src_ref=hidden.at[batch(m), other_half], dst_ref=hv.at[0, batch(m)], send_sem=hid_send.at[m],
                recv_sem=hid_recv.at[m], device_id={"section": 1 - core}, device_id_type=MESH,
            ).wait_send()
        pltpu.make_async_remote_copy(
            src_ref=gains.at[:, other_half], dst_ref=gain_of.at[0], send_sem=gain_send, recv_sem=gain_sem.at[1],
            device_id={"section": 1 - core}, device_id_type=MESH,
        ).wait_send()

    quad = [{"row": 1 - row}, {"section": 1 - core}, {"row": 1 - row, "section": 1 - core}]
    block_rows, block_cols = 16, 512
    lane = lax.broadcasted_iota(jnp.int32, (block_rows, 128), 1)

    def spread(values):
        result = jnp.zeros((block_rows, 128), f32)
        for index, value in enumerate(values):
            result = jnp.where(lane == index, value, result)
        return result

    def row_blocks(m, body):
        @pl.loop(0, row_count // block_rows)
        def _(index):
            body(pl.ds(pl.multiple_of(m * row_count + index * block_rows, block_rows), block_rows))

    def column_blocks():
        for index in range(half // block_cols):
            here = pl.ds(index * block_cols, block_cols)
            there = pl.ds(pl.multiple_of(core * half + index * block_cols, block_cols), block_cols)
            yield here, steer[0:1, there]

    def row_sum(value):
        return jnp.sum(value, -1, keepdims=True)

    def turned(m, there):
        for block in range(row_count // 128):
            at = slice(m * row_count + block * 128, m * row_count + (block + 1) * 128)
            there[0, :, at] = jnp.transpose(sums_of[at, :])[:8]

    def statistics(m):
        def body(at):
            sums = [jnp.zeros((block_rows, block_cols), f32) for _ in range(4)]
            for here, vector in column_blocks():
                for section in range(2):
                    plain = hv[section, at, here].astype(f32)
                    moved = plain + vector
                    sums[2 * section] += plain * plain
                    sums[2 * section + 1] += moved * moved
            sums_of[at, :] = spread([row_sum(value) for value in sums])

        row_blocks(m, body)
        turned(m, stat)
        for index, peer in enumerate(quad):
            Send(stat.at[0, :, batch(m)], stat.at[index + 1, :, batch(m)], stat_send.at[m, index], stat_recv.at[m, index], peer)

    def statistics_wait(m):
        for index in range(3):
            arrived(stat.at[index + 1, :, batch(m)], stat_recv.at[m, index])

    def load_upstream(m):
        pltpu.make_async_copy(u.at[batch(m), my_half], got.at[0, batch(m)], u_sem.at[m]).start()

    curve_sends = {}

    def curvature(section, m):
        incoming = got.at[0] if section == 1 else xc.at[my_block]
        for send in curve_sends.get(m, []):
            send.wait_send()

        def body(at):
            steered = lay[at, 0:1] == float(section)
            curved = jnp.zeros((block_rows, block_cols), f32)
            inner = jnp.zeros((block_rows, block_cols), f32)
            for here, vector in column_blocks():
                plain = hv[section, at, here].astype(f32)
                moved = plain + vector
                scaled = gain_of[section, 0:1, here] * total[at, here]
                curved += scaled * jnp.where(steered, moved, plain)
                inner += incoming[at, here].astype(f32) * moved
            sums_of[at, :] = spread([row_sum(curved), row_sum(inner)])

        row_blocks(m, body)
        turned(m, curve)
        curve_sends[m] = [
            Send(
                curve.at[0, :, batch(m)], curve.at[index + 1, :, batch(m)], curve_send.at[section, m, index],
                curve_recv.at[section, m, index], peer,
            )
            for index, peer in enumerate(quad)
        ]

    def gradient(section, m, out):
        for index in range(3):
            arrived(curve.at[index + 1, :, batch(m)], curve_recv.at[section, m, index])
        if section == 1:
            statistics_wait(m)
        span = 128
        for block in range(row_count // span):
            at = slice(m * row_count + block * span, m * row_count + (block + 1) * span)
            both = (curve[0, :, at] + curve[1, :, at]) + (curve[2, :, at] + curve[3, :, at])
            sums = (stat[0, :, at] + stat[1, :, at]) + (stat[2, :, at] + stat[3, :, at])
            curved, inner = both[0:1], both[1:2]
            plain_sq, moved_sq = sums[2 * section : 2 * section + 1], sums[2 * section + 1 : 2 * section + 2]
            steered = lay_row[0:1, at] == float(section)
            norm_plain = jnp.sqrt(plain_sq + epsilon)
            norm_moved = jnp.sqrt(moved_sq + epsilon)
            rescale = norm_plain / norm_moved
            square_sum = jnp.where(
                steered, norm_plain * norm_plain * moved_sq / (norm_moved * norm_moved), plain_sq
            )
            root_mean = jnp.sqrt(square_sum / D + epsilon)
            scale = jnp.where(steered, rescale, 1.0)
            factor = scale * curved / (D * (root_mean * root_mean * root_mean))
            radial = (inner + curved / root_mean - rescale * factor * moved_sq) / norm_moved
            wide = lax.broadcasted_iota(jnp.int32, (span, span), 0)
            result = jnp.zeros((span, span), f32)
            terms = (1.0 / root_mean, scale * factor, rescale, radial / norm_moved, radial / norm_plain)
            for place, value in enumerate(terms):
                result = jnp.where(wide == place, value, result)
            coef[at, :] = jnp.transpose(result)

        incoming = got.at[0] if section == 1 else xc.at[my_block]

        def body(at):
            steered = lay[at, 0:1] == float(section)
            inverse, pull, rescale, along, back = [coef[at, place : place + 1] for place in range(5)]
            for here, vector in column_blocks():
                plain = hv[section, at, here].astype(f32)
                moved = plain + vector
                scaled = gain_of[section, 0:1, here] * total[at, here]
                grad = incoming[at, here].astype(f32) + scaled * inverse - jnp.where(steered, moved, plain) * pull
                tangent = rescale * (grad - moved * along)
                out[at, here] = jnp.where(steered, tangent + plain * back, grad).astype(jnp.bfloat16)
                kept = jnp.where(steered, tangent, 0.0)
                steer_acc[:, here] += kept[:8] + kept[8:]

        row_blocks(m, body)
        @pl.when(core == section)
        def _():
            pltpu.make_async_copy(out.at[batch(m)], res.at[batch(m), my_half], out_sem.at[0, m]).start()

        @pl.when(core != section)
        def _():
            pltpu.make_async_remote_copy(
                src_ref=out.at[batch(m)], dst_ref=res.at[batch(m), my_half], send_sem=out_send.at[m], recv_sem=out_sem.at[1, m],
                device_id={"section": 1 - core}, device_id_type=MESH,
            ).start()

    def out_wait(section, m):
        pltpu.make_async_remote_copy(
            src_ref=partial.at[0, batch(m)], dst_ref=res.at[batch(m), my_half], send_sem=out_send.at[m], recv_sem=out_sem.at[1, m],
            device_id={"section": 1 - core}, device_id_type=MESH,
        ).wait_send()

    def pass_down(m):
        ref = xc.at[my_block, batch(m)]
        Send(ref, ref, p_send.at[m, 0], p_recv.at[m, 0], {"row": 1 - row})
        Send(ref, ref, p_send.at[m, 1], p_recv.at[m, 1], {"section": 1 - core})

    def pass_on(m):
        ref = xc.at[(1 - row) * 2 + core, batch(m)]
        arrived(ref, p_recv.at[m, 0])
        Send(ref, ref, p_send.at[m, 2], p_recv.at[m, 2], {"section": 1 - core})

    def pass_wait(m):
        arrived(xc.at[row * 2 + 1 - core, batch(m)], p_recv.at[m, 1])
        arrived(xc.at[(1 - row) * 2 + 1 - core, batch(m)], p_recv.at[m, 2])

    def section_one(m):
        finish(m)
        for send in token_sends:
            send.wait_send()
        pltpu.make_async_copy(u.at[batch(m), my_half], got.at[0, batch(m)], u_sem.at[m]).wait()
        curvature(1, m)
        gradient(1, m, xc.at[my_block])
        pass_down(m)

    width = chunk
    own_tiles = half // width

    def early_tile(index):
        rest = jnp.maximum(index - own_tiles, 0)
        source = (col + 1 + rest // 4) % cols
        inside = rest % 4
        start = (inside // 2) * part + (inside % 2) * width
        own = index < own_tiles
        return jnp.where(own, col, source), jnp.where(own, index * width, start)

    def late_tile(k):
        def tile_of(index):
            return (col + 1 + index // 2) % cols, (index % 2) * part + k * width

        return tile_of

    def products(batches, count, tile_of, first):
        def load(index, own=False):
            source, start = tile_of(index)
            slot = index % 2
            rows = pl.ds(pl.multiple_of(start, width), width)
            return pltpu.make_async_copy(
                w.at[rows] if own else wg.at[source, rows],
                w1.at[pl.ds(pl.multiple_of(slot * width, width), width)],
                tile_sem.at[slot],
            )

        def load_start(index, when):
            own = (core == 0) & (index < own_tiles) if first else None
            if own is None:
                pl.when(when)(lambda: load(index).start())
            else:
                pl.when(when & own)(lambda: load(index, True).start())
                pl.when(when & jnp.logical_not(own))(lambda: load(index).start())

        load_start(jnp.int32(0), core >= 0)

        @pl.loop(0, count)
        def _(index):
            load_start(index + 1, index + 1 < count)
            load(index).wait()
            source, start = tile_of(index)
            rows = pl.ds(pl.multiple_of((index % 2) * width, width), width)
            at = pl.ds(pl.multiple_of(start, width), width)
            for m in batches:
                value = lax.dot_general(
                    xc[source, batch(m), :], w1[rows, :], (((1,), (1,)), ((), ())), preferred_element_type=f32
                )
                if first:
                    @pl.when(index < own_tiles)
                    def _():
                        total[batch(m), at] = value

                    @pl.when(index >= own_tiles)
                    def _():
                        total[batch(m), at] += value
                else:
                    total[batch(m), at] += value

    early_count = own_tiles + 12
    steer_acc[...] = jnp.zeros_like(steer_acc)

    first = send_x1(0)
    to_col(0, True)
    wait_own(0)
    for kind in ("in", "mid_own", "out_own"):
        weights_to(kind, 0)
    first.wait_send()
    send_x1(1)
    wait_x1(0)
    to_col(0, False)
    hidden_copies()
    wait_x1(1)
    for send in column_sends:
        send.wait_send()
    for index in (1, 2, last):
        to_col(index, True)
        to_col(index, False)
    gather(0)
    weights_to("in", 1)
    weights_to("mid_own", 1)
    weights_to("out_own", 1)
    hidden_wait()
    statistics(0)
    gather(1)
    gather_rest(0)
    wait_w1(0)
    wait_w1(1)
    multiply(0)
    end_sum(0, 0)
    weights_in(0, 0, "end")
    weights_in(1, 0, "mid")
    end_sum(0, 1)
    gather(2)
    gather(last)
    gather_rest(1)
    multiply(1)
    weights_to("out_own", 2)
    gather_rest(2)
    multiply(2)
    gather_rest(last)
    multiply(last)
    end_sum(1, 0)
    mid_sum(0, 0)
    load_upstream(0)
    weights_in(0, 0, "mid")
    weights_in(0, 1, "end")
    statistics(1)
    weights_to("out_own", 3)
    end_sum(1, 1)
    mid_sum(0, 1)
    load_upstream(1)
    weights_in(1, 1, "mid")
    weights_to("mid_own", 2)
    weights_to("out_far", 0)
    mid_sum(2, 0)
    weights_to("in", 2)
    mid_sum(1, 0)
    weights_in(0, 1, "mid")
    weights_in(0, 2, "end")
    weights_to("out_far", 1)
    end_sum(2, 0)
    weights_to("mid_end", 0)
    mid_sum(2, 1)
    mid_sum(1, 1)
    weights_in(1, 2, "mid")
    weights_in(0, 3, "end")
    weights_to("out_far", 2)
    end_sum(2, 1)
    weights_to("mid_own", 3)
    weights_in(0, 2, "mid")
    weights_in(1, 0, "end")
    weights_in(2, 0, "mid")
    weights_to("out_end", 0)
    weights_to("in", 3)
    weights_to("mid_end", 1)
    section_one(0)
    weights_in(1, 1, "end")
    weights_in(1, 3, "mid")
    weights_to("out_far", 3)
    weights_to("mid_end", 2)
    section_one(1)
    pass_on(0)
    weights_in(1, 2, "end")
    weights_in(2, 1, "mid")
    weights_to("out_end", 1)
    weights_in(0, 3, "mid")
    weights_to("mid_end", 3)
    weights_in(2, 0, "end")
    pass_on(1)
    weights_in(2, 2, "mid")
    weights_to("out_end", 2)
    weights_in(1, 3, "end")
    wait_own(1)
    pass_wait(0)
    weights_in(2, 1, "end")
    for k in range(2):
        for slot in range(3):
            y_arrived(slot, k)
    products([0], early_count, early_tile, True)
    weights_in(2, 3, "mid")
    weights_to("out_end", 3)
    weights_in(2, 2, "end")
    pass_wait(1)
    products([1], early_count, early_tile, True)
    for slot in range(3):
        y_arrived(slot, 2)
    products([0, 1], 6, late_tile(2), False)
    weights_in(2, 3, "end")
    for slot in range(3):
        y_arrived(slot, 3)
    products([0, 1], 6, late_tile(3), False)
    for m in range(micro):
        for send in sum_sends[m]:
            send.wait_send()
    for m in range(micro):
        pl.when(core == 0)(lambda: out_wait(1, m))
        curvature(0, m)
    for m in range(micro):
        gradient(0, m, partial.at[0])

    own_copy = pltpu.make_async_copy(steer_acc, steer_all.at[col], s_local)
    own_copy.start()
    for step in range(1, cols):
        there = (col + step) % cols
        Send(steer_acc, steer_all.at[col], s_send.at[step], s_recv.at[step], {"col": there})
    own_copy.wait()
    for step in range(1, cols):
        arrived(steer_all.at[(col - step) % cols], s_recv.at[step])
    for send in late:
        send.wait_send()
    steer_acc[...] = (steer_all[0] + steer_all[1]) + (steer_all[2] + steer_all[3])
    final = pltpu.make_async_copy(steer_acc, steer_out.at[core], t_sem.at[0])
    final.start()
    give = pltpu.make_async_remote_copy(
        src_ref=steer_acc, dst_ref=steer_out.at[core], send_sem=t_send, recv_sem=t_sem.at[1],
        device_id={"section": 1 - core}, device_id_type=MESH,
    )
    give.start()
    final.wait()
    give.wait()

    for order in range(2):
        pltpu.make_async_remote_copy(
            src_ref=w.at[pl.ds(0, part)], dst_ref=wg.at[col, pl.ds(0, part)], send_sem=half_send.at[order],
            recv_sem=own_sem.at[order], device_id={"section": 1 - core}, device_id_type=MESH,
        ).wait_send()
    hidden_sent()
    for m in range(micro):
        pltpu.make_async_copy(partial.at[0, batch(m)], res.at[batch(m), my_half], out_sem.at[0, m]).wait()
        arrived(res.at[batch(m), other_half], out_sem.at[1, m])
        pl.when(core == 1)(lambda: out_wait(0, m))


def relay(u, w, hidden, gains, steer, lay, lay_row):
    tokens, features = u.shape
    micro = 2
    half = features // 2
    dma = pltpu.SemaphoreType.DMA
    bf16, f32 = jnp.bfloat16, jnp.float32
    in_vmem = pl.BlockSpec(memory_space=pltpu.VMEM)
    anywhere = pl.BlockSpec(memory_space=pl.ANY)
    return pl.pallas_call(
        relay_kernel,
        out_shape=(
            jax.ShapeDtypeStruct((tokens, features), bf16),
            jax.ShapeDtypeStruct((2, 8, half), f32),
            jax.ShapeDtypeStruct((4, half, half), bf16),
            jax.ShapeDtypeStruct((tokens // 4, features), bf16),
        ),
        in_specs=[anywhere, anywhere, anywhere, anywhere, in_vmem, in_vmem, in_vmem],
        out_specs=(anywhere,) * 4,
        scratch_shapes=[
            pltpu.VMEM((4, tokens, half), bf16),
            pltpu.VMEM((half, half), bf16),
            pltpu.VMEM((3, tokens, half), bf16),
            pltpu.VMEM((tokens, half), f32),
            pltpu.VMEM((5, tokens, half), bf16),
            pltpu.VMEM((2, tokens, half), bf16),
            pltpu.VMEM((2, 8, half), f32),
            pltpu.VMEM((tokens, 128), f32),
            pltpu.VMEM((4, 8, tokens), f32),
            pltpu.VMEM((4, 8, tokens), f32),
            pltpu.VMEM((tokens, 128), f32),
            pltpu.VMEM((8, half), f32),
            pltpu.VMEM((4, 8, half), f32),
            dma((2,)), dma((2,)), dma((2,)),
            dma((2,)), dma((2,)),
            dma((3, 2)), dma((4,)), dma,
            dma((4,)), dma((4,)), dma((4,)), dma((4,)), dma((4,)), dma((4,)),
            dma((6, CHUNKS)), dma((3, CHUNKS)), dma((3, CHUNKS)), dma((3, CHUNKS)),
            dma((3, 2, 2)), dma((5, 2)),
            dma((2,)), dma((2,)), dma((2,)), dma((2,)), dma,
            dma((2, 3)), dma((2, 3)),
            dma((2, 2, 3)), dma((2, 2, 3)),
            dma((2,)),
            dma((2, 3)), dma((2, 3)),
            dma((2,)),
            dma((2, 2)), dma((2,)),
            dma((4,)), dma((4,)), dma, dma((2,)), dma,
        ],
        compiler_params=pltpu.CompilerParams(
            collective_id=0, has_side_effects=True, vmem_limit_bytes=63 * 1024 * 1024
        ),
        cost_estimate=pl.CostEstimate(
            flops=4 * 4 * tokens * half * half, bytes_accessed=150 * 1024 * 1024, transcendentals=0
        ),
        name="relay",
    )(u, w, hidden, gains, steer, lay, lay_row)


def shared_weights(hidden, upstream, weights, norm_gains, steering, steer_layer):
    micro, row_count, features = upstream.shape
    tokens = micro * row_count
    f32 = jnp.float32
    gains = jnp.broadcast_to(norm_gains[0].astype(f32), (8, features))
    steer = jnp.broadcast_to(steering.astype(f32), (8, features))
    lay = jnp.broadcast_to(steer_layer.reshape(tokens).astype(f32)[:, None], (tokens, 128))
    lay_row = jnp.broadcast_to(steer_layer.reshape(tokens).astype(f32), (8, tokens))
    result, steer_parts, _, _ = relay(
        upstream.reshape(tokens, features), weights[0], hidden[0].reshape(tokens, features), gains, steer, lay, lay_row
    )
    steer_total = jnp.sum(steer_parts, 1).reshape(features)
    return (result.reshape(1, micro, row_count, features), steer_total / (MICRO * ROWS))


def solution(mesh):
    placed = (
        P("section", None, ("groups", "col"), "row"),
        P(None, ("groups", "col"), "row"),
        P("section", "row", "col"),
        P("section", "row"),
        P(("groups", "row")),
        P(None, ("groups", "col")),
    )
    small = mesh.shape["row"] == 2 and mesh.shape["col"] == 4 and mesh.shape["groups"] == 2
    return jax.shard_map(
        shared_weights if small else local,
        mesh=mesh,
        in_specs=placed,
        out_specs=(P("section", None, ("groups", "col"), "row"), P(("groups", "row"))),
        check_vma=False,
    )
```
